512 devices in a mesh: gx: 4 (over x), gy: 64 (over z, y), gz: 2 (over core).
Axes of the slice: x: 4, y: 8, z: 8, core: 2. Of those that a mesh axis runs over, the one named last changes fastest.
Arguments:
- positions: float32 [3, 524288], P(None, ('gx', 'gy', 'gz')), as said below
- polarizability: float32 [4, 2, 524288], P(None, None, ('gx', 'gy', 'gz')), may hold values from -0.5 to 1
- applied_field: float32 [4, 2, 3, 524288], P(None, None, None, ('gx', 'gy', 'gz')), may hold values from -6 to 6
- pair_codes: int32 [12288], P(('gx', 'gy', 'gz')), may hold values from 0 to 1151
- pair_counts: int32 [512], P(('gx', 'gy', 'gz')), may hold values from 3 to 24, as said below
Outputs:
- dipoles: float32 [4, 2, 3, 524288], P(None, None, None, ('gx', 'gy', 'gz'))
The draws below stay inside these ranges and needn't reach their ends.
Inputs may be any that keep to these rules, and one draw needn't show every extreme that they name: `pair_codes`: each code is ((dx + 1) * 3 + (dy + 1)) * 2 * 8^2 + zt * 8^2 + target_block * 8 + source_block with dx, dy in -1..1, zt in 0..1 and blocks in 0..7; only the first pair_counts entries of a device's list are live. `pair_counts`: some device has 24 live entries in every draw. `positions`: x and y lie in [0, 4) within the owner's slab cell; z lies in [2 z_half, 2 z_half + 2) for the owner's depth half.
All inputs are finite; a program needn't handle non-finite values.
Results may differ from the reference program's by a relative error of at most 0.0003.
Values sent between devices are 32-bit elements; how exact they have to be, the bound alone decides.
No kernel may reach another device: no remote copies, remote signals or barrier semaphores. Data moves between devices by JAX's collectives and lax.ppermute only.
A program may use at most 64 MiB of HBM per device.

```python
import math
import jax
import jax.numpy as jnp
from jax import lax

BLOCK = 128
BLOCKS = 8
FREQS = 4
ITERS = 4
PAIRS = 24
PARTICLES = 524288
N_GX = 4
N_GY = 64
N_GZ = 2
DEVICES = 512


cell_width = 4.0


half_depth = 2.0


def draw_positions(key, part):
    count = BLOCKS * BLOCK * DEVICES
    uniform_draw = jax.random.uniform(key, (3, count), jnp.float32)
    owner_half = (jnp.arange(count, dtype=jnp.int32) // (BLOCKS * BLOCK) % N_GZ).astype(jnp.float32)
    plane = uniform_draw[:2] * cell_width
    across = (uniform_draw[2] + owner_half) * half_depth
    return jnp.concatenate([plane, across[None, :]], axis=0)


def draw_pair_counts(key, part):
    key_base, key_crowd, key_pick = jax.random.split(key, 3)
    base_counts = jax.random.randint(key_base, (DEVICES,), PAIRS // 8, PAIRS // 3 + 1)
    crowded = jax.random.randint(key_crowd, (DEVICES,), 0, 8) == 0
    chosen = jax.random.randint(key_pick, (), 0, DEVICES)
    crowded = crowded | (jnp.arange(DEVICES, dtype=jnp.int32) == chosen)
    return jnp.where(crowded, PAIRS, base_counts).astype(jnp.int32)


def touch_ends(drawn, key, low, top_value):
    extent = drawn.shape
    place = [jax.random.randint(jax.random.fold_in(key, axis), (), 0, extent[axis]) for axis in range(len(extent))]
    drawn = drawn.at[tuple(place)].set(low)
    longest = extent.index(max(extent))
    place[longest] = (place[longest] + 1) % extent[longest]
    return drawn.at[tuple(place)].set(top_value)


def block_scale(own_key, extent, cuts, smallest, top_value):
    factor_of = 1.0
    for axis_at, shards_of in cuts:
        steps = jax.random.uniform(jax.random.fold_in(jax.random.fold_in(own_key, 6), axis_at), (shards_of,), jnp.float32, smallest / len(cuts), top_value / len(cuts))
        factor_of = factor_of * jnp.repeat(jnp.exp(steps), extent[axis_at] // shards_of).reshape((-1,) + (1,) * (len(extent) - 1 - axis_at))
    return factor_of


def normal_values(own_key, shape, deviation, reach, cuts=(), kind=jnp.bfloat16):
    level = block_scale(own_key, shape, cuts, -0.22, 0.18) if cuts else 1.0
    values = jax.random.normal(own_key, shape, jnp.float32) * deviation * level
    return jnp.minimum(jnp.maximum(values, -reach), reach).astype(kind)


def setup_inputs(seed: int = 0) -> dict:
    seeds = jax.random.split(jax.random.key(seed), 6)
    return {
        "positions": draw_positions(jax.random.fold_in(seeds[5], 71), 0),
        "polarizability": jnp.clip(-0.5 + 1.5 * jax.random.uniform(seeds[1], (FREQS, 2, PARTICLES), jnp.float32) ** block_scale(seeds[1], (FREQS, 2, PARTICLES), ((2, 512),), -0.2, 0.2), -0.5, 1.0),
        "applied_field": normal_values(seeds[2], (FREQS, 2, 3, PARTICLES), 1.0, 6.0, ((3, 512),), jnp.float32),
        "pair_codes": touch_ends(jax.random.randint(seeds[3], (N_GX * N_GY * N_GZ * PAIRS,), 0, 18 * BLOCKS * BLOCKS), jax.random.fold_in(seeds[3], 1), 0, (18 * BLOCKS * BLOCKS) - 1).astype(jnp.int32),
        "pair_counts": draw_pair_counts(jax.random.fold_in(seeds[5], 71), 0),
    }


cell_width = 4.0
soften = 1.0
screen = 0.5
coupling = 0.8

def tensor_field(tgt_pos, src_pos, shift_x, shift_y, sources):
    disp_x = tgt_pos[0][:, None] - src_pos[0][None, :] + shift_x
    disp_y = tgt_pos[1][:, None] - src_pos[1][None, :] + shift_y
    disp_z = tgt_pos[2][:, None] - src_pos[2][None, :]
    dist_sq = disp_x * disp_x + disp_y * disp_y + disp_z * disp_z + soften * soften
    inv_dist = lax.rsqrt(dist_sq)
    distance = dist_sq * inv_dist
    screened = jax.scipy.special.erfc(screen * distance)
    gaussian = 2.0 * screen / math.sqrt(math.pi) * jnp.exp(-screen * screen * dist_sq)
    inv_sq = inv_dist * inv_dist
    b_term = screened * inv_sq * inv_dist + gaussian * inv_sq
    c_term = (3.0 * screened * inv_sq * inv_dist + gaussian * (2.0 * screen * screen + 3.0 * inv_sq)) * inv_sq
    disp_vec = jnp.stack([disp_x, disp_y, disp_z])
    tensor = c_term[None, :, None, :] * disp_vec[:, :, None, :] * jnp.transpose(disp_vec, (1, 0, 2))[None, :, :, :]
    tensor = tensor - jnp.eye(3, dtype=tensor.dtype)[:, None, :, None] * b_term[None, :, None, :]
    block_len = tgt_pos.shape[1]
    matrix = tensor.reshape(3 * block_len, 3 * block_len)
    flat_src = sources.reshape(-1, 3 * block_len)
    result = lax.dot_general(flat_src, matrix, (((1,), (1,)), ((), ())), precision=lax.Precision.HIGHEST, preferred_element_type=jnp.float32)
    return result.reshape(sources.shape)

def reference(positions, polarizability, applied_field, pair_codes, pair_counts):
    freqs = polarizability.shape[0]
    device_count = N_GX * N_GY * N_GZ
    block_count = BLOCKS * device_count
    pos_blocks = positions.reshape(3, block_count, BLOCK).transpose(1, 0, 2)
    alpha_blocks = polarizability.reshape(freqs, 2, block_count, BLOCK).transpose(2, 0, 1, 3)
    field_blocks = applied_field.reshape(freqs, 2, 3, block_count, BLOCK).transpose(3, 0, 1, 2, 4)
    a_re = alpha_blocks[:, :, 0][:, :, None]
    a_im = alpha_blocks[:, :, 1][:, :, None]

    def respond(field_re, field_im):
        return jnp.stack([a_re * field_re - a_im * field_im, a_re * field_im + a_im * field_re], axis=2)
    square = BLOCKS * BLOCKS

    def induced(dipoles):

        def per_device(total, device):
            slab_x = device // (N_GY * N_GZ)
            slab_y = device // N_GZ % N_GY
            depth = device % N_GZ
            pair_list = lax.dynamic_slice_in_dim(pair_codes, (device * PAIRS).astype(jnp.int32), PAIRS)
            pair_total = pair_counts[device]
            src_block = pair_list % BLOCKS
            tgt_block = pair_list // BLOCKS % BLOCKS
            depth_tgt = pair_list // square % 2
            step_y = pair_list // (2 * square) % 3 - 1
            step_x = pair_list // (6 * square) - 1
            src_index = (((slab_x + step_x) % N_GX * N_GY + slab_y) * N_GZ + depth) * BLOCKS + src_block
            tgt_index = ((slab_x * N_GY + (slab_y + step_y) % N_GY) * N_GZ + depth_tgt) * BLOCKS + tgt_block
            shift_x = -step_x.astype(jnp.float32) * cell_width
            shift_y = step_y.astype(jnp.float32) * cell_width
            contrib = jax.vmap(tensor_field)(pos_blocks[tgt_index], pos_blocks[src_index], shift_x, shift_y, dipoles[src_index])
            active = (jnp.arange(PAIRS, dtype=jnp.int32) < pair_total).astype(jnp.float32)
            return (total.at[tgt_index].add(contrib * active[:, None, None, None, None]), None)
        total, unused = lax.scan(per_device, jnp.zeros_like(dipoles), jnp.arange(device_count, dtype=jnp.int32))
        return total
    dipoles = respond(field_blocks[:, :, 0], field_blocks[:, :, 1])
    for sweep in range(ITERS):
        field = induced(dipoles)
        dipoles = respond(field_blocks[:, :, 0] + coupling * field[:, :, 0], field_blocks[:, :, 1] + coupling * field[:, :, 1])
    return dipoles.transpose(1, 2, 3, 0, 4).reshape(freqs, 2, 3, block_count * BLOCK)
```

```python
import functools
import math

import jax
import jax.numpy as jnp
from jax import lax
from jax.experimental import pallas as pl
from jax.experimental.pallas import tpu as pltpu
from jax.sharding import PartitionSpec as P

BLOCK = 128
ITERS = 4

cell_width = 4.0
coupling = 0.8
root_pi = 1.0 / math.sqrt(math.pi)
erfcx_fit = (
    1.790011536,
    0.928601473,
    0.3238769782,
    0.05183749415,
    -0.01103335474,
    -0.006028563159,
    0.0006207049413,
    0.0006951546236,
    -6.044884693e-05,
    -6.930253734e-05,
)

VMEM = pl.BlockSpec(memory_space=pltpu.VMEM)
SMEM = pl.BlockSpec(memory_space=pltpu.SMEM)


def swaps(count, first):
    if first:
        return [(i, i ^ 1) for i in range(count)]
    return [(i, (i + 1) % count if i % 2 else (i - 1) % count) for i in range(count)]


def exchange(value, axis):
    count = lax.axis_size(axis)
    return (
        lax.ppermute(value, axis, swaps(count, True)),
        lax.ppermute(value, axis, swaps(count, False)),
    )


def rows_of(value, block):
    return value[:, pl.ds(pl.multiple_of(block * BLOCK, BLOCK), BLOCK)]


def lower_half(shape):
    return lax.broadcasted_iota(jnp.int32, shape, 0) % 8 < 4


def build(word, src_slot, spos, tpos, tens):
    entry = word & 63
    src_block = (word >> 6) & 7
    half = (word >> 9) & 1
    tgt_block = (word >> 10) & 7
    tgt_half = (word >> 13) & 1
    tgt_slot = (word >> 14) & 3
    shift_x = (((word >> 16) & 3) - 1).astype(jnp.float32) * -cell_width
    shift_y = (((word >> 18) & 3) - 1).astype(jnp.float32) * cell_width
    src = spos.at[src_slot * 2 + half]
    src_cols = pl.ds(pl.multiple_of(src_block * BLOCK, BLOCK), BLOCK)
    tgt_cols = pl.ds(pl.multiple_of(tgt_block * BLOCK, BLOCK), BLOCK)
    sx, sy, sz = (src[k : k + 1, src_cols] for k in range(3))
    tgt = jnp.transpose(tpos[tgt_slot * 2 + tgt_half, :, tgt_cols])
    chunk = 32
    for start in range(0, BLOCK, chunk):
        part = tgt[start : start + chunk]
        dx = part[:, 0:1] - sx + shift_x
        dy = part[:, 1:2] - sy + shift_y
        dz = part[:, 2:3] - sz
        dist_sq = dx * dx + dy * dy + dz * dz + 1.0
        inv_dist = lax.rsqrt(dist_sq)
        distance = dist_sq * inv_dist
        inv_sq = inv_dist * inv_dist
        reach = 1.0 / (distance + 4.0)
        at = reach * 10.0 - 1.0
        fit = jnp.full_like(at, erfcx_fit[-1])
        for coef in erfcx_fit[-2::-1]:
            fit = fit * at + coef
        decay = jnp.exp(dist_sq * -0.25)
        b_term = inv_sq * decay * (fit * reach * inv_dist + root_pi)
        c_term = inv_sq * (3.0 * b_term + (0.5 * root_pi) * decay)
        cx, cy, cz = c_term * dx, c_term * dy, c_term * dz
        comps = (cx * dx - b_term, cx * dy, cx * dz, cy * dy - b_term, cy * dz, cz * dz - b_term)
        for k, comp in enumerate(comps):
            high = comp.astype(jnp.bfloat16)
            low = (comp - high.astype(jnp.float32)).astype(jnp.bfloat16)
            tens[entry, pl.ds(k * BLOCK + start, chunk), 0:BLOCK] = high
            tens[entry, pl.ds(k * BLOCK + start, chunk), BLOCK : 2 * BLOCK] = low


def apply(word, dip, tens, out, self_target):
    entry = word & 63
    src_block = (word >> 6) & 7
    half = (word >> 9) & 1
    tgt_block = (word >> 10) & 7
    tgt_half = (word >> 13) & 1
    tgt_slot = (word >> 14) & 3
    cols = pl.ds(pl.multiple_of(src_block * BLOCK, BLOCK), BLOCK)
    value = dip[0:24, cols]
    mine = (lax.broadcasted_iota(jnp.int32, (24, BLOCK), 0) % 8 // 4) == half
    high = value.astype(jnp.bfloat16).astype(jnp.float32)
    low = value - high
    low = jnp.concatenate([pltpu.roll(low[8 * k : 8 * k + 8], 4, 0) for k in range(3)], axis=0)
    left = jnp.where(mine, high, low)
    right = jnp.where(mine, high, 0.0)
    lhs = jnp.concatenate([left, right], axis=1).astype(jnp.bfloat16)
    res = lax.dot_general(
        lhs, tens[entry], (((1,), (1,)), ((), ())), preferred_element_type=jnp.float32
    )
    pick = ((0, 1, 2), (1, 3, 4), (2, 4, 5))
    outcols = pl.ds(pl.multiple_of(tgt_block * BLOCK, BLOCK), BLOCK)
    place = tgt_half if self_target else (tgt_slot - 1) * 2 + tgt_half
    for a in range(3):
        total = out[place, 8 * a : 8 * a + 8, outcols]
        for b in range(3):
            k = pick[a][b]
            total = total + res[8 * b : 8 * b + 8, k * BLOCK : (k + 1) * BLOCK]
        out[place, 8 * a : 8 * a + 8, outcols] = total


def each(tab, group, body):
    base = group * 64

    def step(i, carry):
        body(tab[base + 1 + i])
        return carry

    lax.fori_loop(0, tab[base], step, 0)


def settle(acc, place, out, out_row=0):
    for a in range(3):
        own, other = acc[place, 8 * a : 8 * a + 8, :], acc[place + 1, 8 * a : 8 * a + 8, :]
        own = own + pltpu.roll(own, 4, 0)
        other = other + pltpu.roll(other, 4, 0)
        out[8 * a : 8 * a + 8, :] = jnp.where(lower_half(own.shape), own, other)


def first_kernel(lists, own, xa, xb, ya, yb, tens, tab, msg_a, msg_b, spos, tpos, acc):
    for group in range(6):
        tab[group * 64] = 0
    core, even_x, even_y = lists[50], lists[51], lists[52]
    for half in range(2):

        def place(p, carry, half=half):
            code = lists[half * 25 + p]
            steps = code >> 7
            step_x = (steps * 11) >> 5
            step_y = steps - 3 * step_x
            slot_x = jnp.where(step_x == 1, 0, jnp.where((step_x == 2) == (even_x == 1), 1, 2))
            slot_y = jnp.where(step_y == 1, 0, jnp.where((step_y == 2) == (even_y == 1), 1, 2))
            tgt_half = ((code >> 6) & 1) ^ core
            word = (
                (half * 24 + p)
                | ((code & 7) << 6)
                | (half << 9)
                | (((code >> 3) & 7) << 10)
                | (tgt_half << 13)
                | (slot_y << 14)
                | (step_x << 16)
                | (step_y << 18)
            )
            group = slot_x + jnp.where(slot_y == 0, 3, 0)
            at = tab[group * 64]
            tab[group * 64 + 1 + at] = word
            tab[group * 64] = at + 1
            return carry

        lax.fori_loop(0, lists[half * 25 + 24], place, 0)
    for slot, (source, target) in enumerate(((own, own), (xa, ya), (xb, yb))):
        base = 24
        for half in range(2):
            spos[slot * 2 + half, 0:3, :] = source[base + 3 * half : base + 3 * half + 3, :]
            row = base if slot == 0 else 0
            tpos[slot * 2 + half, 0:3, :] = target[row + 3 * half : row + 3 * half + 3, :]
    acc[...] = jnp.zeros_like(acc)
    for slot, dip in enumerate((own, xa, xb)):

        def both(word, slot=slot, dip=dip):
            build(word, slot, spos, tpos, tens)
            apply(word, dip, tens, acc, False)

        each(tab, slot, both)
    settle(acc, 0, msg_a)
    settle(acc, 2, msg_b)


def second_kernel(tab, own, xa, xb, tens_in, field, tens, spos, acc):
    for slot, source in enumerate((own, xa, xb)):
        for half in range(2):
            spos[slot * 2 + half, 0:3, :] = source[24 + 3 * half : 27 + 3 * half, :]
    acc[...] = jnp.zeros_like(acc)
    for slot, dip in enumerate((own, xa, xb)):

        def both(word, slot=slot, dip=dip):
            build(word, slot, spos, spos, tens)
            apply(word, dip, tens, acc, True)

        each(tab, slot + 3, both)
    settle(acc, 0, field)


def local_kernel(tab, own, tens, acc_far, acc_near):
    acc_far[...] = jnp.zeros_like(acc_far)
    acc_near[...] = jnp.zeros_like(acc_near)
    each(tab, 0, lambda word: apply(word, own, tens, acc_far, False))
    each(tab, 3, lambda word: apply(word, own, tens, acc_near, True))


def far_kernel(tab, xa, xb, tens, acc_in, msg_a, msg_b, acc):
    acc[...] = acc_in[...]
    each(tab, 1, lambda word: apply(word, xa, tens, acc, False))
    each(tab, 2, lambda word: apply(word, xb, tens, acc, False))
    settle(acc, 0, msg_a)
    settle(acc, 2, msg_b)


def near_kernel(tab, xa, xb, tens, acc_in, field, acc):
    acc[...] = acc_in[...]
    each(tab, 4, lambda word: apply(word, xa, tens, acc, True))
    each(tab, 5, lambda word: apply(word, xb, tens, acc, True))
    settle(acc, 0, field)


def respond_rows(alpha, total):
    real_row = lax.broadcasted_iota(jnp.int32, (8, total.shape[1]), 0) % 4 < 2
    turned = jnp.where(real_row, pltpu.roll(total, 6, 0), pltpu.roll(total, 2, 0))
    return alpha[0:8] * total + alpha[8:16] * turned


def update_kernel(field, from_a, from_b, applied, alpha, dip):
    for a in range(3):
        rows = slice(8 * a, 8 * a + 8)
        total = applied[rows, :] + coupling * (field[rows, :] + from_a[rows, :] + from_b[rows, :])
        dip[rows, :] = respond_rows(alpha[...], total)


def start_kernel(applied, alpha, pos, dip):
    for a in range(3):
        rows = slice(8 * a, 8 * a + 8)
        dip[rows, :] = respond_rows(alpha[...], applied[rows, :])
    dip[24:32, :] = pos[...]


def call(body, out_shape, scratch=(), in_specs=None, out_specs=None, aliases=None):
    specs = {} if in_specs is None else {"in_specs": in_specs, "out_specs": out_specs}
    return pl.pallas_call(
        body,
        out_shape=out_shape,
        **specs,
        scratch_shapes=list(scratch),
        input_output_aliases=aliases or {},
        compiler_params=pltpu.CompilerParams(vmem_limit_bytes=16 * 1024 * 1024),
    )


def shards(positions, polarizability, applied_field, pair_codes, pair_counts):
    rows = positions.shape[1]
    entries = pair_codes.shape[0]
    half_freqs = polarizability.shape[0] // 2
    core = lax.axis_index("gz")
    f32 = jnp.float32
    arr = lambda r: jax.ShapeDtypeStruct((r, rows), f32)
    pack = lambda f, a: jnp.concatenate(
        [
            jnp.transpose(f, (2, 1, 0, 3)).reshape(12, rows),
            jnp.transpose(a, (1, 0, 2)).reshape(4, rows),
        ],
        axis=0,
    )
    freqs_of = lambda v, c: lax.dynamic_slice_in_dim(v, c * half_freqs, half_freqs, 0)
    mine = pack(freqs_of(applied_field, core), freqs_of(polarizability, core))
    theirs = pack(freqs_of(applied_field, 1 - core), freqs_of(polarizability, 1 - core))
    codes = jnp.concatenate([pair_codes, pair_counts])
    codes_row = jnp.pad(codes.astype(f32), (0, rows - entries - 1))[None]
    sent = jnp.concatenate([theirs, positions, codes_row], axis=0)
    got = lax.ppermute(sent, "gz", swaps(2, True))
    join = lambda u, v, k: jnp.stack([u.reshape(k, 4, rows), v.reshape(k, 4, rows)], axis=1).reshape(8 * k, rows)
    applied = join(mine[:12], got[:12], 3)
    base = join(mine[12:16], got[12:16], 1).reshape(2, 2, 2, rows)
    real = jnp.broadcast_to(base[:, :1], base.shape).reshape(8, rows)
    imag = base[:, 1:]
    imag = jnp.concatenate([-imag, imag], axis=1).reshape(8, rows)
    alpha = jnp.concatenate([real, imag], axis=0)
    pos = jnp.concatenate([positions, got[16:19], jnp.zeros((2, rows), f32)], axis=0)
    parity = lambda axis: 1 - lax.axis_index(axis) % 2
    lists = jnp.concatenate(
        [
            codes,
            got[19, : entries + 1].astype(jnp.int32),
            jnp.stack([core, parity("gx"), parity("gy")]).astype(jnp.int32),
        ]
    )
    ya, yb = exchange(pos, "gy")
    own = call(start_kernel, arr(32))(applied, alpha, pos)
    xa, xb = exchange(own, "gx")
    tens_shape = pltpu.VMEM((2 * entries, 6 * BLOCK, 2 * BLOCK), jnp.bfloat16)
    keep = lambda v: pltpu.with_memory_space_constraint(v, pltpu.VMEM)
    tab_shape = jax.ShapeDtypeStruct((6 * 64,), jnp.int32)
    far_shape = jax.ShapeDtypeStruct((4, 24, rows), f32)
    near_shape = jax.ShapeDtypeStruct((2, 24, rows), f32)
    far_scratch = pltpu.VMEM((4, 24, rows), f32)
    near_scratch = pltpu.VMEM((2, 24, rows), f32)
    pos_scratch = pltpu.VMEM((6, 8, rows), f32)
    tens, tab, msg_a, msg_b = call(
        first_kernel,
        (tens_shape, tab_shape, arr(24), arr(24)),
        (pos_scratch, pos_scratch, far_scratch),
        [SMEM] + [VMEM] * 5,
        (VMEM, SMEM, VMEM, VMEM),
    )(lists, own, xa, xb, ya, yb)
    from_a, from_b = swap_back(msg_a, msg_b)
    field, tens = call(
        second_kernel,
        (arr(24), tens_shape),
        (pos_scratch, near_scratch),
        [SMEM] + [VMEM] * 4,
        (VMEM, VMEM),
        {4: 1},
    )(tab, own, xa, xb, keep(tens))
    dip = call(update_kernel, arr(24))(field, from_a, from_b, applied, alpha)
    for sweep in range(1, ITERS):
        xa, xb = exchange(dip, "gx")
        far, near = call(
            local_kernel, (far_shape, near_shape), (), [SMEM] + [VMEM] * 2, (VMEM, VMEM)
        )(tab, dip, keep(tens))
        msg_a, msg_b = call(
            far_kernel, (arr(24), arr(24)), (far_scratch,), [SMEM] + [VMEM] * 4, (VMEM, VMEM)
        )(tab, xa, xb, keep(tens), far)
        from_a, from_b = swap_back(msg_a, msg_b)
        field = call(near_kernel, arr(24), (near_scratch,), [SMEM] + [VMEM] * 4, VMEM)(
            tab, xa, xb, keep(tens), near
        )
        dip = call(update_kernel, arr(24))(field, from_a, from_b, applied, alpha)
    dip = dip.reshape(3, 2, 2, half_freqs, rows)
    kept = jnp.transpose(dip[:, 0], (2, 1, 0, 3))
    passed = lax.ppermute(jnp.transpose(dip[:, 1], (2, 1, 0, 3)), "gz", swaps(2, True))
    return jnp.where(
        core == 0, jnp.concatenate([kept, passed]), jnp.concatenate([passed, kept])
    )


def swap_back(msg_a, msg_b):
    count = lax.axis_size("gy")
    return (
        lax.ppermute(msg_a, "gy", swaps(count, True)),
        lax.ppermute(msg_b, "gy", swaps(count, False)),
    )


def solution(mesh):
    in_specs = (
        P(None, ("gx", "gy", "gz")),
        P(None, None, ("gx", "gy", "gz")),
        P(None, None, None, ("gx", "gy", "gz")),
        P(("gx", "gy", "gz")),
        P(("gx", "gy", "gz")),
    )
    out_specs = P(None, None, None, ("gx", "gy", "gz"))
    return jax.shard_map(shards, mesh=mesh, in_specs=in_specs, out_specs=out_specs, check_vma=False)
```

```python
import functools
import math

import jax
import jax.numpy as jnp
from jax import lax
from jax.experimental import pallas as pl
from jax.experimental.pallas import tpu as pltpu
from jax.sharding import PartitionSpec as P

BLOCK = 128
ITERS = 4

cell_width = 4.0
coupling = 0.8
root_pi = 1.0 / math.sqrt(math.pi)
erfcx_fit = (
    1.790011536,
    0.928601473,
    0.3238769782,
    0.05183749415,
    -0.01103335474,
    -0.006028563159,
    0.0006207049413,
    0.0006951546236,
    -6.044884693e-05,
    -6.930253734e-05,
)

VMEM = pl.BlockSpec(memory_space=pltpu.VMEM)
SMEM = pl.BlockSpec(memory_space=pltpu.SMEM)


def swaps(count, first):
    if first:
        return [(i, i ^ 1) for i in range(count)]
    return [(i, (i + 1) % count if i % 2 else (i - 1) % count) for i in range(count)]


def exchange(value, axis):
    count = lax.axis_size(axis)
    return (
        lax.ppermute(value, axis, swaps(count, True)),
        lax.ppermute(value, axis, swaps(count, False)),
    )


def rows_of(value, block):
    return value[:, pl.ds(pl.multiple_of(block * BLOCK, BLOCK), BLOCK)]


def lower_half(shape):
    return lax.broadcasted_iota(jnp.int32, shape, 0) % 8 < 4


def build(word, spos, tpos, tens):
    entry = word & 63
    src_block = (word >> 6) & 7
    half = (word >> 9) & 1
    tgt_block = (word >> 10) & 7
    tgt_half = (word >> 13) & 1
    tgt_slot = (word >> 14) & 3
    shift_x = (((word >> 16) & 3) - 1).astype(jnp.float32) * -cell_width
    shift_y = (((word >> 18) & 3) - 1).astype(jnp.float32) * cell_width
    src_slot = (word >> 20) & 3
    src = spos.at[src_slot * 2 + half]
    src_cols = pl.ds(pl.multiple_of(src_block * BLOCK, BLOCK), BLOCK)
    tgt_cols = pl.ds(pl.multiple_of(tgt_block * BLOCK, BLOCK), BLOCK)
    tgt = tpos.at[tgt_slot * 2 + tgt_half]
    tx, ty, tz = (tgt[k : k + 1, tgt_cols] for k in range(3))
    source = jnp.transpose(src[:, src_cols])
    chunk = 32
    for start in range(0, BLOCK, chunk):
        part = source[start : start + chunk]
        dx = tx - part[:, 0:1] + shift_x
        dy = ty - part[:, 1:2] + shift_y
        dz = tz - part[:, 2:3]
        dist_sq = dx * dx + dy * dy + dz * dz + 1.0
        inv_dist = lax.rsqrt(dist_sq)
        distance = dist_sq * inv_dist
        inv_sq = inv_dist * inv_dist
        reach = 1.0 / (distance + 4.0)
        at = reach * 10.0 - 1.0
        fit = jnp.full_like(at, erfcx_fit[-1])
        for coef in erfcx_fit[-2::-1]:
            fit = fit * at + coef
        decay = jnp.exp(dist_sq * -0.25)
        b_term = inv_sq * decay * (fit * reach * inv_dist + root_pi)
        c_term = inv_sq * (3.0 * b_term + (0.5 * root_pi) * decay)
        cx, cy, cz = c_term * dx, c_term * dy, c_term * dz
        comps = (cx * dx - b_term, cx * dy, cx * dz, cy * dy - b_term, cy * dz, cz * dz - b_term)
        for k, comp in enumerate(comps):
            high = comp.astype(jnp.bfloat16)
            low = (comp - high.astype(jnp.float32)).astype(jnp.bfloat16)
            cols = slice(k * BLOCK, (k + 1) * BLOCK)
            tens[entry, start : start + chunk, cols] = high
            tens[entry, BLOCK + start : BLOCK + start + chunk, cols] = low


def apply(words, counts, dips, tens, out):
    results = []
    for word, live in zip(words, counts):
        entry = word & 63
        src_block = (word >> 6) & 7
        half = (word >> 9) & 1
        cols = pl.ds(pl.multiple_of(src_block * BLOCK, BLOCK), BLOCK)
        row_half = lax.broadcasted_iota(jnp.int32, (8, BLOCK), 0) % 8 // 4
        src_slot = (word >> 20) & 3
        mine = row_half == half
        left, right = [], []
        for k in range(3):
            value = dips[src_slot, 8 * k : 8 * k + 8, cols]
            if live is not None:
                value = jnp.where(live, value, 0.0)
            high = value.astype(jnp.bfloat16).astype(jnp.float32)
            low = pltpu.roll(value - high, 4, 0)
            left.append(jnp.where(mine, high, low))
            right.append(jnp.where(mine, high, 0.0))
        lhs = jnp.concatenate(
            [jnp.concatenate(left, axis=0), jnp.concatenate(right, axis=0)], axis=1
        ).astype(jnp.bfloat16)
        results.append(
            lax.dot_general(
                lhs, tens[entry], (((1,), (0,)), ((), ())), preferred_element_type=jnp.float32
            )
        )
    pick = ((0, 1, 2), (1, 3, 4), (2, 4, 5))
    for word, res in zip(words, results):
        tgt_block = (word >> 10) & 7
        tgt_half = (word >> 13) & 1
        outcols = pl.ds(pl.multiple_of(tgt_block * BLOCK, BLOCK), BLOCK)
        for a in range(3):
            total = res[0:8, pick[a][0] * BLOCK : (pick[a][0] + 1) * BLOCK]
            for b in (1, 2):
                k = pick[a][b]
                total = total + res[8 * b : 8 * b + 8, k * BLOCK : (k + 1) * BLOCK]
            out[tgt_half, 8 * a : 8 * a + 8, outcols] += total


def each_build(tab, group, spos, tpos, tens):
    base = group * 64
    count = tab[base]

    def step(i, carry):
        for j in range(2):
            build(tab[base + 1 + jnp.minimum(2 * i + j, count - 1)], spos, tpos, tens)
        return carry

    lax.fori_loop(0, (count + 1) // 2, step, 0)


def each_apply(tab, group, dips, tens, out):
    base = group * 64
    count = tab[base]

    def step(i, carry):
        words, live = [], []
        for j in range(4):
            at = 4 * i + j
            words.append(tab[base + 1 + jnp.minimum(at, count - 1)])
            live.append(None if j == 0 else at < count)
        apply(words, live, dips, tens, out)
        return carry

    lax.fori_loop(0, (count + 3) // 4, step, 0)


def settle(acc, out):
    for a in range(3):
        rows = slice(8 * a, 8 * a + 8)
        own, other = acc[0, rows, :], acc[1, rows, :]
        own = own + pltpu.roll(own, 4, 0)
        other = other + pltpu.roll(other, 4, 0)
        out[rows, :] = jnp.where(lower_half(own.shape), own, other)


def sort_entries(lists, tab):
    for group in range(6):
        tab[group * 64] = 0
    core, even_x, even_y = lists[50], lists[51], lists[52]
    for half in range(2):

        def place(p, carry, half=half):
            code = lists[half * 25 + p]
            steps = code >> 7
            step_x = (steps * 11) >> 5
            step_y = steps - 3 * step_x
            slot_x = jnp.where(step_x == 1, 0, jnp.where((step_x == 2) == (even_x == 1), 1, 2))
            slot_y = jnp.where(step_y == 1, 0, jnp.where((step_y == 2) == (even_y == 1), 1, 2))
            tgt_half = ((code >> 6) & 1) ^ core
            word = (
                (half * 24 + p)
                | ((code & 7) << 6)
                | (half << 9)
                | (((code >> 3) & 7) << 10)
                | (tgt_half << 13)
                | (slot_y << 14)
                | (step_x << 16)
                | (step_y << 18)
                | (slot_x << 20)
            )
            group = slot_y + jnp.where(slot_x == 0, 0, 3)
            at = tab[group * 64]
            tab[group * 64 + 1 + at] = word
            tab[group * 64] = at + 1
            return carry

        lax.fori_loop(0, lists[half * 25 + 24], place, 0)


def stack_dipoles(dips, arrays):
    for slot, value in arrays:
        dips[slot] = value[0:24, :]


def stack_positions(place, arrays):
    for slot, value, row in arrays:
        for half in range(2):
            place[slot * 2 + half, 0:3, :] = value[row + 3 * half : row + 3 * half + 3, :]


def first_local_kernel(lists, own, ya, yb, tens, tab, here, at_a, at_b, dips, spos, tpos):
    sort_entries(lists, tab)
    stack_dipoles(dips, ((0, own),))
    stack_positions(spos, ((0, own, 24),))
    stack_positions(tpos, ((0, own, 24), (1, ya, 0), (2, yb, 0)))
    for group in range(3):
        each_build(tab, group, spos, tpos, tens)
    for group, out in enumerate((here, at_a, at_b)):
        out[...] = jnp.zeros_like(out)
        each_apply(tab, group, dips, tens, out)


def local_kernel(tab, own, tens, here, at_a, at_b, dips):
    stack_dipoles(dips, ((0, own),))
    for group, out in enumerate((here, at_a, at_b)):
        out[...] = jnp.zeros_like(out)
        each_apply(tab, group, dips, tens, out)


def first_rest_kernel(group, tab, xa, xb, target, tens_in, begun, out, tens, dips, spos, tpos, acc):
    stack_dipoles(dips, ((1, xa), (2, xb)))
    stack_positions(spos, ((1, xa, 24), (2, xb, 24)))
    stack_positions(tpos, ((group, target, 0 if group else 24),))
    acc[...] = begun[...]
    each_build(tab, 3 + group, spos, tpos, tens)
    each_apply(tab, 3 + group, dips, tens, acc)
    settle(acc, out)


def rest_kernel(group, tab, xa, xb, tens, begun, out, dips, acc):
    stack_dipoles(dips, ((1, xa), (2, xb)))
    acc[...] = begun[...]
    each_apply(tab, 3 + group, dips, tens, acc)
    settle(acc, out)


def respond_rows(alpha, total):
    real_row = lax.broadcasted_iota(jnp.int32, (8, total.shape[1]), 0) % 4 < 2
    turned = jnp.where(real_row, pltpu.roll(total, 6, 0), pltpu.roll(total, 2, 0))
    return alpha[0:8] * total + alpha[8:16] * turned


def update_kernel(field, from_a, from_b, applied, alpha, dip):
    for a in range(3):
        rows = slice(8 * a, 8 * a + 8)
        total = applied[rows, :] + coupling * (field[rows, :] + from_a[rows, :] + from_b[rows, :])
        dip[rows, :] = respond_rows(alpha[...], total)


def last_kernel(field, from_a, from_b, applied, alpha, kept, passed):
    for a in range(3):
        rows = slice(8 * a, 8 * a + 8)
        total = applied[rows, :] + coupling * (field[rows, :] + from_a[rows, :] + from_b[rows, :])
        dip = respond_rows(alpha[...], total)
        for i in range(2):
            for f in range(2):
                at = 2 * i + f
                kept[f, i, a : a + 1, :] = dip[at : at + 1]
                passed[f, i, a : a + 1, :] = dip[4 + at : 5 + at]


def pack_kernel(lists, positions, polarizability, applied, sent, mine):
    core = lists[25]
    for out, first in ((mine, 2 * core), (sent, 2 - 2 * core)):
        for i in range(2):
            for f in range(2):
                for a in range(3):
                    row = 4 * a + 2 * i + f
                    out[row : row + 1, :] = applied[first + f, i, a : a + 1, :]
                row = 12 + 2 * i + f
                out[row : row + 1, :] = polarizability[first + f, i : i + 1, :]
    sent[16:19, :] = positions[...]
    lane = lax.broadcasted_iota(jnp.int32, (1, BLOCK), 1)
    codes = jnp.zeros((1, BLOCK), jnp.int32)
    for p in range(25):
        codes = jnp.where(lane == p, lists[p], codes)
    sent[19:24, :] = jnp.zeros((5, sent.shape[1]), jnp.float32)
    sent[19:20, 0:BLOCK] = codes.astype(jnp.float32)


def join_kernel(mine, got, positions, applied, alpha, pos, own):
    for half, value in enumerate((mine, got)):
        for a in range(3):
            applied[8 * a + 4 * half : 8 * a + 4 * half + 4, :] = value[4 * a : 4 * a + 4, :]
        real, imag = value[12:14, :], value[14:16, :]
        alpha[4 * half : 4 * half + 2, :] = real
        alpha[4 * half + 2 : 4 * half + 4, :] = real
        alpha[8 + 4 * half : 10 + 4 * half, :] = -imag
        alpha[10 + 4 * half : 12 + 4 * half, :] = imag
    pos[0:3, :] = positions[...]
    pos[3:6, :] = got[16:19, :]
    pos[6:8, :] = jnp.zeros((2, pos.shape[1]), jnp.float32)
    for a in range(3):
        rows = slice(8 * a, 8 * a + 8)
        own[rows, :] = respond_rows(alpha[...], applied[rows, :])
    own[24:32, :] = pos[...]


def call(body, out_shape, scratch=(), in_specs=None, out_specs=None, aliases=None):
    specs = {} if in_specs is None else {"in_specs": in_specs, "out_specs": out_specs}
    return pl.pallas_call(
        body,
        out_shape=out_shape,
        **specs,
        scratch_shapes=list(scratch),
        input_output_aliases=aliases or {},
        compiler_params=pltpu.CompilerParams(vmem_limit_bytes=16 * 1024 * 1024),
    )


def shards(positions, polarizability, applied_field, pair_codes, pair_counts):
    rows = positions.shape[1]
    entries = pair_codes.shape[0]
    core = lax.axis_index("gz")
    f32 = jnp.float32
    arr = lambda *shape: jax.ShapeDtypeStruct((*shape, rows), f32)
    held = lambda *shape: pltpu.VMEM((*shape, rows), f32)
    parity = lambda axis: 1 - lax.axis_index(axis) % 2
    turn = lambda value, first: lax.ppermute(value, "gy", swaps(lax.axis_size("gy"), first))
    codes = jnp.concatenate([pair_codes, pair_counts])
    place = jnp.stack([core, parity("gx"), parity("gy")]).astype(jnp.int32)
    sent, mine = call(
        pack_kernel, (arr(24), arr(16)), (), [SMEM] + [VMEM] * 3, (VMEM, VMEM)
    )(jnp.concatenate([codes, place]), positions, polarizability, applied_field)
    got = lax.ppermute(sent, "gz", swaps(2, True))
    applied, alpha, pos, own = call(join_kernel, (arr(24), arr(16), arr(8), arr(32)))(
        mine, got, positions
    )
    lists = jnp.concatenate([codes, got[19, : entries + 1].astype(jnp.int32), place])
    yb = turn(pos, False)
    ya = turn(pos, True)
    xa, xb = exchange(own, "gx")
    tens_shape = pltpu.VMEM((2 * entries, 2 * BLOCK, 6 * BLOCK), jnp.bfloat16)
    keep = lambda v: pltpu.with_memory_space_constraint(v, pltpu.VMEM)
    tab_shape = jax.ShapeDtypeStruct((6 * 64,), jnp.int32)
    dip_scratch, pos_scratch, acc_scratch = held(3, 24), held(6, 8), held(2, 24)
    sums = (arr(2, 24),) * 3
    tens, tab, here, at_a, at_b = call(
        first_local_kernel,
        (tens_shape, tab_shape, *sums),
        (dip_scratch, pos_scratch, pos_scratch),
        [SMEM] + [VMEM] * 3,
        (VMEM, SMEM, VMEM, VMEM, VMEM),
    )(lists, own, ya, yb)

    def first_rest(group, target, tens, begun):
        return call(
            functools.partial(first_rest_kernel, group),
            (arr(24), tens_shape),
            (dip_scratch, pos_scratch, pos_scratch, acc_scratch),
            [SMEM] + [VMEM] * 5,
            (VMEM, VMEM),
            {4: 1},
        )(tab, xa, xb, target, keep(tens), begun)

    def rest(group, xa, xb, begun):
        return call(
            functools.partial(rest_kernel, group),
            arr(24),
            (dip_scratch, acc_scratch),
            [SMEM] + [VMEM] * 4,
            VMEM,
        )(tab, xa, xb, keep(tens), begun)

    msg_b, tens = first_rest(2, yb, tens, at_b)
    from_b = turn(msg_b, False)
    msg_a, tens = first_rest(1, ya, tens, at_a)
    from_a = turn(msg_a, True)
    field, tens = first_rest(0, own, tens, here)
    for sweep in range(1, ITERS):
        dip = call(update_kernel, arr(24))(field, from_a, from_b, applied, alpha)
        xa, xb = exchange(dip, "gx")
        here, at_a, at_b = call(
            local_kernel, sums, (dip_scratch,), [SMEM] + [VMEM] * 2, (VMEM,) * 3
        )(tab, dip, keep(tens))
        from_b = turn(rest(2, xa, xb, at_b), False)
        from_a = turn(rest(1, xa, xb, at_a), True)
        field = rest(0, xa, xb, here)
    half = jax.ShapeDtypeStruct((2, 2, 3, rows), f32)
    kept, passed = call(last_kernel, (half, half))(field, from_a, from_b, applied, alpha)
    passed = lax.ppermute(passed, "gz", swaps(2, True))
    return jnp.where(
        core == 0, jnp.concatenate([kept, passed]), jnp.concatenate([passed, kept])
    )


def solution(mesh):
    in_specs = (
        P(None, ("gx", "gy", "gz")),
        P(None, None, ("gx", "gy", "gz")),
        P(None, None, None, ("gx", "gy", "gz")),
        P(("gx", "gy", "gz")),
        P(("gx", "gy", "gz")),
    )
    out_specs = P(None, None, None, ("gx", "gy", "gz"))
    return jax.shard_map(shards, mesh=mesh, in_specs=in_specs, out_specs=out_specs, check_vma=False)
```

```python
import functools
import math

import jax
import jax.numpy as jnp
from jax import lax
from jax.experimental import pallas as pl
from jax.experimental.pallas import tpu as pltpu
from jax.sharding import PartitionSpec as P

BLOCK = 128
ITERS = 4

cell_width = 4.0
coupling = 0.8
root_pi = 1.0 / math.sqrt(math.pi)
erfcx_fit = (
    1.790011536,
    0.928601473,
    0.3238769782,
    0.05183749415,
    -0.01103335474,
    -0.006028563159,
    0.0006207049413,
    0.0006951546236,
    -6.044884693e-05,
    -6.930253734e-05,
)

VMEM = pl.BlockSpec(memory_space=pltpu.VMEM)
SMEM = pl.BlockSpec(memory_space=pltpu.SMEM)
SLABS = 4
KEPT = 72
STRIDE = 256


def swaps(count, first):
    if first:
        return [(i, i ^ 1) for i in range(count)]
    return [(i, (i + 1) % count if i % 2 else (i - 1) % count) for i in range(count)]


def columns(block):
    return pl.ds(pl.multiple_of(block * BLOCK, BLOCK), BLOCK)


def build(word, src_pos, tgt_pos, tens, slot):
    src_slab = (word >> 11) & 3
    tgt_slab = (word >> 16) & 3
    shift_x = (((word >> 18) & 3) - 1).astype(jnp.float32) * -cell_width
    shift_y = (((word >> 20) & 3) - 1).astype(jnp.float32) * cell_width
    tgt_cols = columns((word >> 13) & 7)
    tx, ty, tz = (tgt_pos[tgt_slab, k : k + 1, tgt_cols] for k in range(3))
    tx, ty = tx + shift_x, ty + shift_y
    source = jnp.transpose(src_pos[src_slab, :, columns((word >> 8) & 7)])
    chunk = 32
    for start in range(0, BLOCK, chunk):
        part = source[start : start + chunk]
        dx = tx - part[:, 0:1]
        dy = ty - part[:, 1:2]
        dz = tz - part[:, 2:3]
        dist_sq = dx * dx + dy * dy + dz * dz + 1.0
        inv_dist = lax.rsqrt(dist_sq)
        distance = dist_sq * inv_dist
        inv_sq = inv_dist * inv_dist
        reach = 1.0 / (distance + 4.0)
        at = reach * 10.0 - 1.0
        fit = jnp.full_like(at, erfcx_fit[-1])
        for coef in erfcx_fit[-2::-1]:
            fit = fit * at + coef
        decay = jnp.exp2(dist_sq * (-0.25 / math.log(2.0)))
        b_term = inv_sq * decay * (fit * reach * inv_dist + root_pi)
        c_term = inv_sq * (3.0 * b_term + (0.5 * root_pi) * decay)
        cx, cy, cz = c_term * dx, c_term * dy, c_term * dz
        comps = (cx * dx - b_term, cx * dy, cx * dz, cy * dy - b_term, cy * dz, cz * dz - b_term)
        for k, comp in enumerate(comps):
            high = comp.astype(jnp.bfloat16)
            low = (comp - high.astype(jnp.float32)).astype(jnp.bfloat16)
            cols = slice(k * BLOCK, (k + 1) * BLOCK)
            tens[slot, start : start + chunk, cols] = high
            tens[slot, BLOCK + start : BLOCK + start + chunk, cols] = low


def apply(words, slots, live, dip, tens, out):
    results = []
    row_slab = lax.broadcasted_iota(jnp.int32, (8, BLOCK), 0) // 2
    for word, slot, ok in zip(words, slots, live):
        src_slab = (word >> 11) & 3
        cols = columns((word >> 8) & 7)
        mine = row_slab == src_slab
        beside = row_slab == ((src_slab + 1) & 3)
        left, right = [], []
        for k in range(3):
            value = dip[8 * k : 8 * k + 8, cols]
            if ok is not None:
                value = jnp.where(ok, value, 0.0)
            high = value.astype(jnp.bfloat16).astype(jnp.float32)
            low = pltpu.roll(value - high, 2, 0)
            part = jnp.where(mine, high, 0.0)
            left.append(jnp.where(beside, low, part))
            right.append(part)
        lhs = jnp.concatenate(
            [jnp.concatenate(left, axis=0), jnp.concatenate(right, axis=0)], axis=1
        ).astype(jnp.bfloat16)
        results.append(
            lax.dot_general(
                lhs, tens[slot], (((1,), (0,)), ((), ())), preferred_element_type=jnp.float32
            )
        )
    pick = ((0, 1, 2), (1, 3, 4), (2, 4, 5))
    for word, res in zip(words, results):
        cols = columns((word >> 13) & 7)
        tgt_slab = (word >> 16) & 3
        for a in range(3):
            total = res[0:8, pick[a][0] * BLOCK : (pick[a][0] + 1) * BLOCK]
            for b in (1, 2):
                k = pick[a][b]
                total = total + res[8 * b : 8 * b + 8, k * BLOCK : (k + 1) * BLOCK]
            out[tgt_slab, 8 * a : 8 * a + 8, cols] += total


def each_build(tab, group, src_pos, tgt_pos, tens):
    base = group * STRIDE
    count = tab[base]

    def step(i, carry):
        for j in range(2):
            word = tab[base + 1 + jnp.minimum(2 * i + j, count - 1)]
            build(word, src_pos, tgt_pos, tens, word & 255)
        return carry

    lax.fori_loop(0, (count + 1) // 2, step, 0)


def each_apply(tab, group, dip, tens, out):
    base = group * STRIDE
    count = tab[base]

    def step(i, carry):
        words, live = [], []
        for j in range(4):
            at = 4 * i + j
            words.append(tab[base + 1 + jnp.minimum(at, count - 1)])
            live.append(None if j == 0 else at < count)
        apply(words, [word & 255 for word in words], live, dip, tens, out)
        return carry

    lax.fori_loop(0, (count + 3) // 4, step, 0)


def each_other(tab, group, src_pos, tgt_pos, dip, out, one):
    base = (group + 6) * STRIDE

    def step(i, carry):
        word = tab[base + 1 + i]
        build(word, src_pos, tgt_pos, one, 0)
        apply([word], [0], [None], dip, one, out)
        return carry

    lax.fori_loop(0, tab[base], step, 0)


def settle(acc, out):
    for a in range(3):
        rows = slice(8 * a, 8 * a + 8)
        joined = None
        for s in range(SLABS):
            part = acc[s, rows, :]
            part = part + pltpu.roll(part, 4, 0)
            part = part + pltpu.roll(part, 2, 0)
            mine = lax.broadcasted_iota(jnp.int32, part.shape, 0) // 2 == s
            joined = part if s == 0 else jnp.where(mine, part, joined)
        out[rows, :] = joined


def sort_entries(lists, tab):
    for group in range(12):
        tab[group * STRIDE] = 0
    core = lax.axis_index("gz")
    odd_y = lax.rem(lax.axis_index("gy"), 2)
    used = jnp.int32(0)
    for half in range(2):
        for slab in range(SLABS):
            which = half * SLABS + slab

            def place(p, used, half=half, slab=slab, which=which):
                code = lists[which, 0, p].astype(jnp.int32)
                steps = code >> 7
                step_x = (steps * 11) >> 5
                step_y = steps - 3 * step_x
                slot_y = jnp.where(step_y == 1, 0, jnp.where((step_y == 2) == (odd_y == 0), 1, 2))
                word = (
                    used
                    | ((code & 7) << 8)
                    | (((slab + step_x + SLABS - 1) & (SLABS - 1)) << 11)
                    | (((code >> 3) & 7) << 13)
                    | (slab << 16)
                    | (step_x << 18)
                    | (step_y << 20)
                )
                group = 3 * half + slot_y + jnp.where(used >= KEPT, 6, 0)
                hit = jnp.where(((code >> 6) & 1) == core, 1, 0)
                at = tab[group * STRIDE]
                tab[group * STRIDE + 1 + at] = word
                tab[group * STRIDE] = at + hit
                return used + hit

            used = lax.fori_loop(0, lists[which, 0, 24].astype(jnp.int32), place, used)


def spread(value, row, out):
    for s in range(SLABS):
        out[s, 0:3, :] = value[row + 3 * s : row + 3 * s + 3, :]


def first_kernel(own, got, tens, tab, own_pos, got_pos, lists, sems):
    copies = []
    for half, value in enumerate((own, got)):
        for s in range(SLABS):
            which = half * SLABS + s
            row = 36 + s
            copies.append(
                pltpu.make_async_copy(
                    value.at[row : row + 1, 0:BLOCK], lists.at[which], sems.at[which]
                )
            )
    for copy in copies:
        copy.start()
    own_pos[...] = jnp.zeros_like(own_pos)
    got_pos[...] = jnp.zeros_like(got_pos)
    spread(own, 24, own_pos)
    spread(got, 24, got_pos)
    for copy in copies:
        copy.wait()
    sort_entries(lists, tab)
    each_build(tab, 0, own_pos, own_pos, tens)
    each_build(tab, 3, got_pos, own_pos, tens)


def first_far_kernel(slot, tab, own, got, own_pos, got_pos, pos, tens_in, out, tens, tgt_pos, acc, one):
    spread(pos, 0, tgt_pos)
    acc[...] = jnp.zeros_like(acc)
    for group, src_pos, dip in ((slot, own_pos, own), (3 + slot, got_pos, got)):
        each_build(tab, group, src_pos, tgt_pos, tens)
        each_apply(tab, group, dip, tens, acc)
        each_other(tab, group, src_pos, tgt_pos, dip, acc, one)
    settle(acc, out)


def own_kernel(tab, own, own_pos, pos_a, pos_b, tens, at_a, at_b, tgt_pos, one):
    for slot, pos, out in ((2, pos_b, at_b), (1, pos_a, at_a)):
        out[...] = jnp.zeros_like(out)
        each_apply(tab, slot, own, tens, out)
        spread(pos, 0, tgt_pos)
        each_other(tab, slot, own_pos, tgt_pos, own, out, one)


def far_kernel(slot, tab, got, got_pos, pos, tens, begun, out, tgt_pos, acc, one):
    acc[...] = begun[...]
    each_apply(tab, 3 + slot, got, tens, acc)
    spread(pos, 0, tgt_pos)
    each_other(tab, 3 + slot, got_pos, tgt_pos, got, acc, one)
    settle(acc, out)


def here_kernel(tab, own, got, own_pos, got_pos, tens, out, acc, one):
    acc[...] = jnp.zeros_like(acc)
    for group, src_pos, dip in ((0, own_pos, own), (3, got_pos, got)):
        each_apply(tab, group, dip, tens, acc)
        each_other(tab, group, src_pos, own_pos, dip, acc, one)
    settle(acc, out)


def respond_rows(alpha, total):
    real_row = lax.broadcasted_iota(jnp.int32, (8, total.shape[1]), 0) % 2 < 1
    turned = jnp.where(real_row, pltpu.roll(total, 7, 0), pltpu.roll(total, 1, 0))
    return alpha[0:8] * total + alpha[8:16] * turned


def update_kernel(field, from_a, from_b, applied, alpha, dip):
    for a in range(3):
        rows = slice(8 * a, 8 * a + 8)
        total = applied[rows, :] + coupling * (field[rows, :] + from_a[rows, :] + from_b[rows, :])
        dip[rows, :] = respond_rows(alpha[...], total)


def last_kernel(field, from_a, from_b, applied, alpha, out):
    out[...] = jnp.zeros_like(out)
    for a in range(3):
        rows = slice(8 * a, 8 * a + 8)
        total = applied[rows, :] + coupling * (field[rows, :] + from_a[rows, :] + from_b[rows, :])
        dip = respond_rows(alpha[...], total)
        for s in range(SLABS):
            for i in range(2):
                out[s, 3 * i + a : 3 * i + a + 1, :] = dip[2 * s + i : 2 * s + i + 1]


def pack_kernel(pos, pol, field, codes, count, out):
    lane = lax.broadcasted_iota(jnp.int32, (1, BLOCK), 1)
    row = jnp.where(lane == codes.shape[0], count[0], 0)
    for p in range(codes.shape[0]):
        row = jnp.where(lane == p, codes[p], row)
    for f in range(SLABS):
        for i in range(2):
            out[f, 3 * i : 3 * i + 3, :] = field[f, i]
        out[f, 6:8, :] = pol[f]
        out[f, 8:16, :] = jnp.zeros((8, out.shape[2]), jnp.float32)
        out[f, 8:11, :] = pos[...]
        out[f, 11:12, 0:BLOCK] = row.astype(jnp.float32)


def join_kernel(got, applied, alpha, own, pos):
    for s in range(SLABS):
        for i in range(2):
            for a in range(3):
                row = 8 * a + 2 * s + i
                applied[row : row + 1, :] = got[s, 3 * i + a : 3 * i + a + 1, :]
        real, imag = got[s, 6:7, :], got[s, 7:8, :]
        alpha[2 * s : 2 * s + 1, :] = real
        alpha[2 * s + 1 : 2 * s + 2, :] = real
        alpha[8 + 2 * s : 9 + 2 * s, :] = -imag
        alpha[9 + 2 * s : 10 + 2 * s, :] = imag
        pos[3 * s : 3 * s + 3, :] = got[s, 8:11, :]
        own[24 + 3 * s : 27 + 3 * s, :] = got[s, 8:11, :]
        own[36 + s : 37 + s, :] = got[s, 11:12, :]
    for a in range(3):
        rows = slice(8 * a, 8 * a + 8)
        own[rows, :] = respond_rows(alpha[...], applied[rows, :])


def call(body, out_shape, scratch=(), in_specs=None, out_specs=None, aliases=None):
    specs = {} if in_specs is None else {"in_specs": in_specs, "out_specs": out_specs}
    return pl.pallas_call(
        body,
        out_shape=out_shape,
        **specs,
        scratch_shapes=list(scratch),
        input_output_aliases=aliases or {},
        compiler_params=pltpu.CompilerParams(vmem_limit_bytes=6 * 1024 * 1024),
    )


def shards(positions, polarizability, applied_field, pair_codes, pair_counts):
    rows = positions.shape[1]
    f32 = jnp.float32
    arr = lambda *shape: jax.ShapeDtypeStruct((*shape, rows), f32)
    held = lambda *shape: pltpu.VMEM((*shape, rows), f32)
    flip = lambda value: lax.ppermute(value, "gz", swaps(2, True))
    turn = lambda value, first: lax.ppermute(value, "gy", swaps(lax.axis_size("gy"), first))
    keep = lambda value: pltpu.with_memory_space_constraint(value, pltpu.VMEM)
    fixed = lambda value: pltpu.with_memory_space_constraint(value, pltpu.SMEM)
    sent = call(pack_kernel, arr(SLABS, 16), (), [VMEM] * 3 + [SMEM] * 2, VMEM)(
        positions, polarizability, applied_field, pair_codes, pair_counts
    )
    got = lax.all_to_all(sent, "gx", 0, 0)
    applied, alpha, own, pos = call(join_kernel, (arr(24), arr(16), arr(40), arr(12)))(got)
    got = flip(own)
    pos_b = turn(pos, False)
    pos_a = turn(pos, True)
    tens_shape = pltpu.VMEM((KEPT, 2 * BLOCK, 6 * BLOCK), jnp.bfloat16)
    one = pltpu.VMEM((1, 2 * BLOCK, 6 * BLOCK), jnp.bfloat16)
    tgt_pos, acc = held(SLABS, 8), held(SLABS, 24)
    tens, tab, own_pos, got_pos = call(
        first_kernel,
        (tens_shape, pltpu.SMEM((12 * STRIDE,), jnp.int32), arr(SLABS, 8), arr(SLABS, 8)),
        (pltpu.SMEM((2 * SLABS, 1, BLOCK), f32), pltpu.SemaphoreType.DMA((2 * SLABS,))),
        [VMEM] * 2,
        (VMEM, SMEM, VMEM, VMEM),
    )(own, got)
    tab = fixed(tab)

    def first_far(slot, pos, tens):
        return call(
            functools.partial(first_far_kernel, slot),
            (arr(24), tens_shape),
            (tgt_pos, acc, one),
            [SMEM] + [VMEM] * 6,
            (VMEM, VMEM),
            {6: 1},
        )(tab, own, got, own_pos, got_pos, pos, keep(tens))

    def here(own, got):
        return call(here_kernel, arr(24), (acc, one), [SMEM] + [VMEM] * 5, VMEM)(
            tab, own, got, own_pos, got_pos, keep(tens)
        )

    def far(slot, got, pos, begun):
        return call(
            functools.partial(far_kernel, slot),
            arr(24),
            (tgt_pos, acc, one),
            [SMEM] + [VMEM] * 5,
            VMEM,
        )(tab, got, got_pos, pos, keep(tens), begun)

    msg, tens = first_far(2, pos_b, tens)
    from_b = turn(msg, False)
    msg, tens = first_far(1, pos_a, tens)
    from_a = turn(msg, True)
    field = here(own, got)
    for sweep in range(1, ITERS):
        own = call(update_kernel, arr(24))(field, from_a, from_b, applied, alpha)
        got = flip(own)
        at_a, at_b = call(
            own_kernel,
            (arr(SLABS, 24), arr(SLABS, 24)),
            (tgt_pos, one),
            [SMEM] + [VMEM] * 5,
            (VMEM, VMEM),
        )(tab, own, own_pos, pos_a, pos_b, keep(tens))
        from_b = turn(far(2, got, pos_b, at_b), False)
        from_a = turn(far(1, got, pos_a, at_a), True)
        field = here(own, got)
    out = call(last_kernel, arr(SLABS, 8))(field, from_a, from_b, applied, alpha)
    out = lax.all_to_all(out, "gx", 0, 0)
    return out[:, :6].reshape(SLABS, 2, 3, rows)


def solution(mesh):
    in_specs = (
        P(None, ("gx", "gy", "gz")),
        P(None, None, ("gx", "gy", "gz")),
        P(None, None, None, ("gx", "gy", "gz")),
        P(("gx", "gy", "gz")),
        P(("gx", "gy", "gz")),
    )
    out_specs = P(None, None, None, ("gx", "gy", "gz"))
    return jax.shard_map(shards, mesh=mesh, in_specs=in_specs, out_specs=out_specs, check_vma=False)
```

```python
import functools
import math

import jax
import jax.numpy as jnp
from jax import lax
from jax.experimental import pallas as pl
from jax.experimental.pallas import tpu as pltpu
from jax.sharding import PartitionSpec as P

BLOCK = 128
ITERS = 4

cell_width = 4.0
coupling = 0.8
root_pi = 1.0 / math.sqrt(math.pi)
erfcx_fit = (
    1.790011536,
    0.928601473,
    0.3238769782,
    0.05183749415,
    -0.01103335474,
    -0.006028563159,
    0.0006207049413,
    0.0006951546236,
    -6.044884693e-05,
    -6.930253734e-05,
)

VMEM = pl.BlockSpec(memory_space=pltpu.VMEM)
SMEM = pl.BlockSpec(memory_space=pltpu.SMEM)
SLABS = 4
KEPT = 72
STRIDE = 256


def swaps(count, first):
    if first:
        return [(i, i ^ 1) for i in range(count)]
    return [(i, (i + 1) % count if i % 2 else (i - 1) % count) for i in range(count)]


def columns(block):
    return pl.ds(pl.multiple_of(block * BLOCK, BLOCK), BLOCK)


def build(word, src_pos, tgt_pos, tens, slot):
    src_slab = (word >> 11) & 3
    tgt_slab = (word >> 16) & 3
    shift_x = (((word >> 18) & 3) - 1).astype(jnp.float32) * -cell_width
    shift_y = (((word >> 20) & 3) - 1).astype(jnp.float32) * cell_width
    tgt_cols = columns((word >> 13) & 7)
    tx, ty, tz = (tgt_pos[tgt_slab, k : k + 1, tgt_cols] for k in range(3))
    tx, ty = tx + shift_x, ty + shift_y
    source = jnp.transpose(src_pos[src_slab, :, columns((word >> 8) & 7)])
    chunk = 32
    for start in range(0, BLOCK, chunk):
        part = source[start : start + chunk]
        dx = tx - part[:, 0:1]
        dy = ty - part[:, 1:2]
        dz = tz - part[:, 2:3]
        dist_sq = dx * dx + dy * dy + dz * dz + 1.0
        inv_dist = lax.rsqrt(dist_sq)
        distance = dist_sq * inv_dist
        inv_sq = inv_dist * inv_dist
        reach = 1.0 / (distance + 4.0)
        at = reach * 10.0 - 1.0
        fit = jnp.full_like(at, erfcx_fit[-1])
        for coef in erfcx_fit[-2::-1]:
            fit = fit * at + coef
        decay = jnp.exp2(dist_sq * (-0.25 / math.log(2.0)))
        b_term = inv_sq * decay * (fit * reach * inv_dist + root_pi)
        c_term = inv_sq * (3.0 * b_term + (0.5 * root_pi) * decay)
        cx, cy, cz = c_term * dx, c_term * dy, c_term * dz
        comps = (cx * dx - b_term, cx * dy, cx * dz, cy * dy - b_term, cy * dz, cz * dz - b_term)
        for k, comp in enumerate(comps):
            high = comp.astype(jnp.bfloat16)
            low = (comp - high.astype(jnp.float32)).astype(jnp.bfloat16)
            cols = slice(k * BLOCK, (k + 1) * BLOCK)
            tens[slot, start : start + chunk, cols] = high
            tens[slot, BLOCK + start : BLOCK + start + chunk, cols] = low


def apply(words, slots, live, dip, tens, out):
    results = []
    row_slab = lax.broadcasted_iota(jnp.int32, (8, BLOCK), 0) // 2
    for word, slot, ok in zip(words, slots, live):
        src_slab = (word >> 11) & 3
        cols = columns((word >> 8) & 7)
        mine = row_slab == src_slab
        beside = row_slab == ((src_slab + 1) & 3)
        left, right = [], []
        for k in range(3):
            value = dip[8 * k : 8 * k + 8, cols]
            if ok is not None:
                value = jnp.where(ok, value, 0.0)
            high = value.astype(jnp.bfloat16).astype(jnp.float32)
            low = pltpu.roll(value - high, 2, 0)
            part = jnp.where(mine, high, 0.0)
            left.append(jnp.where(beside, low, part))
            right.append(part)
        lhs = jnp.concatenate(
            [jnp.concatenate(left, axis=0), jnp.concatenate(right, axis=0)], axis=1
        ).astype(jnp.bfloat16)
        results.append(
            lax.dot_general(
                lhs, tens[slot], (((1,), (0,)), ((), ())), preferred_element_type=jnp.float32
            )
        )
    pick = ((0, 1, 2), (1, 3, 4), (2, 4, 5))
    for word, res in zip(words, results):
        cols = columns((word >> 13) & 7)
        tgt_slab = (word >> 16) & 3
        for a in range(3):
            total = res[0:8, pick[a][0] * BLOCK : (pick[a][0] + 1) * BLOCK]
            for b in (1, 2):
                k = pick[a][b]
                total = total + res[8 * b : 8 * b + 8, k * BLOCK : (k + 1) * BLOCK]
            out[tgt_slab, 8 * a : 8 * a + 8, cols] += total


def each_build(tab, group, src_pos, tgt_pos, tens):
    base = group * STRIDE
    count = tab[base]

    def step(i, carry):
        for j in range(2):
            word = tab[base + 1 + jnp.minimum(2 * i + j, count - 1)]
            build(word, src_pos, tgt_pos, tens, word & 255)
        return carry

    lax.fori_loop(0, (count + 1) // 2, step, 0)


def each_apply(tab, group, dip, tens, out):
    base = group * STRIDE
    count = tab[base]

    def step(i, carry):
        words, live = [], []
        for j in range(4):
            at = 4 * i + j
            words.append(tab[base + 1 + jnp.minimum(at, count - 1)])
            live.append(None if j == 0 else at < count)
        apply(words, [word & 255 for word in words], live, dip, tens, out)
        return carry

    lax.fori_loop(0, (count + 3) // 4, step, 0)


def each_other(tab, group, src_pos, tgt_pos, dip, out, one):
    base = (group + 6) * STRIDE

    def step(i, carry):
        word = tab[base + 1 + i]
        build(word, src_pos, tgt_pos, one, 0)
        apply([word], [0], [None], dip, one, out)
        return carry

    lax.fori_loop(0, tab[base], step, 0)


def settle(acc, out):
    for a in range(3):
        rows = slice(8 * a, 8 * a + 8)
        joined = None
        for s in range(SLABS):
            part = acc[s, rows, :]
            part = part + pltpu.roll(part, 4, 0)
            part = part + pltpu.roll(part, 2, 0)
            mine = lax.broadcasted_iota(jnp.int32, part.shape, 0) // 2 == s
            joined = part if s == 0 else jnp.where(mine, part, joined)
        out[rows, :] = joined


def sort_entries(lists, tab):
    for group in range(12):
        tab[group * STRIDE] = 0
    core = lax.axis_index("gz")
    odd_y = lax.rem(lax.axis_index("gy"), 2)
    used = jnp.int32(0)
    for half in range(2):
        for slab in range(SLABS):
            which = half * SLABS + slab

            def place(p, used, half=half, slab=slab, which=which):
                code = lists[which, 0, p].astype(jnp.int32)
                steps = code >> 7
                step_x = (steps * 11) >> 5
                step_y = steps - 3 * step_x
                slot_y = jnp.where(step_y == 1, 0, jnp.where((step_y == 2) == (odd_y == 0), 1, 2))
                word = (
                    used
                    | ((code & 7) << 8)
                    | (((slab + step_x + SLABS - 1) & (SLABS - 1)) << 11)
                    | (((code >> 3) & 7) << 13)
                    | (slab << 16)
                    | (step_x << 18)
                    | (step_y << 20)
                )
                group = 3 * half + slot_y + jnp.where(used >= KEPT, 6, 0)
                hit = jnp.where(((code >> 6) & 1) == core, 1, 0)
                at = tab[group * STRIDE]
                tab[group * STRIDE + 1 + at] = word
                tab[group * STRIDE] = at + hit
                return used + hit

            used = lax.fori_loop(0, lists[which, 0, 24].astype(jnp.int32), place, used)


def spread(value, row, out):
    for s in range(SLABS):
        out[s, 0:3, :] = value[row + 3 * s : row + 3 * s + 3, :]


def first_kernel(own, got, tens, tab, own_pos, got_pos, lists, sems):
    copies = []
    for half, value in enumerate((own, got)):
        for s in range(SLABS):
            which = half * SLABS + s
            row = 36 + s
            copies.append(
                pltpu.make_async_copy(
                    value.at[row : row + 1, 0:BLOCK], lists.at[which], sems.at[which]
                )
            )
    for copy in copies:
        copy.start()
    own_pos[...] = jnp.zeros_like(own_pos)
    got_pos[...] = jnp.zeros_like(got_pos)
    spread(own, 24, own_pos)
    spread(got, 24, got_pos)
    for copy in copies:
        copy.wait()
    sort_entries(lists, tab)
    each_build(tab, 0, own_pos, own_pos, tens)


def first_far_kernel(slot, tab, own, got, own_pos, got_pos, pos, tens_in, out, tens, tgt_pos, acc, one):
    spread(pos, 0, tgt_pos)
    acc[...] = jnp.zeros_like(acc)
    for group, src_pos, dip in ((slot, own_pos, own), (3 + slot, got_pos, got)):
        each_build(tab, group, src_pos, tgt_pos, tens)
        each_apply(tab, group, dip, tens, acc)
        each_other(tab, group, src_pos, tgt_pos, dip, acc, one)
    settle(acc, out)


def own_kernel(tab, own, own_pos, pos_a, pos_b, tens, at_a, at_b, tgt_pos, one):
    for slot, pos, out in ((2, pos_b, at_b), (1, pos_a, at_a)):
        out[...] = jnp.zeros_like(out)
        each_apply(tab, slot, own, tens, out)
        spread(pos, 0, tgt_pos)
        each_other(tab, slot, own_pos, tgt_pos, own, out, one)


def far_kernel(slot, tab, got, got_pos, pos, tens, begun, out, tgt_pos, acc, one):
    acc[...] = begun[...]
    each_apply(tab, 3 + slot, got, tens, acc)
    spread(pos, 0, tgt_pos)
    each_other(tab, 3 + slot, got_pos, tgt_pos, got, acc, one)
    settle(acc, out)


def here_kernel(tab, own, got, own_pos, got_pos, tens, out, acc, one):
    acc[...] = jnp.zeros_like(acc)
    for group, src_pos, dip in ((0, own_pos, own), (3, got_pos, got)):
        each_apply(tab, group, dip, tens, acc)
        each_other(tab, group, src_pos, own_pos, dip, acc, one)
    settle(acc, out)


def first_here_kernel(tab, own, got, own_pos, got_pos, tens_in, out, tens, acc, one):
    each_build(tab, 3, got_pos, own_pos, tens)
    here_kernel(tab, own, got, own_pos, got_pos, tens, out, acc, one)


def respond_rows(alpha, total):
    real_row = lax.broadcasted_iota(jnp.int32, (8, total.shape[1]), 0) % 2 < 1
    turned = jnp.where(real_row, pltpu.roll(total, 7, 0), pltpu.roll(total, 1, 0))
    return alpha[0:8] * total + alpha[8:16] * turned


def update_kernel(field, from_a, from_b, applied, alpha, dip):
    for a in range(3):
        rows = slice(8 * a, 8 * a + 8)
        total = applied[rows, :] + coupling * (field[rows, :] + from_a[rows, :] + from_b[rows, :])
        dip[rows, :] = respond_rows(alpha[...], total)


def last_kernel(field, from_a, from_b, applied, alpha, out):
    for a in range(3):
        rows = slice(8 * a, 8 * a + 8)
        total = applied[rows, :] + coupling * (field[rows, :] + from_a[rows, :] + from_b[rows, :])
        dip = respond_rows(alpha[...], total)
        for s in range(SLABS):
            out[s, a] = dip[2 * s : 2 * s + 2]


def pack_kernel(pos_in, pol_in, field_in, codes_in, count, out, pos, pol, field, codes, sems):
    pairs = ((field_in, field), (pol_in, pol), (pos_in, pos), (codes_in, codes))
    copies = [pltpu.make_async_copy(a, b, sems.at[k]) for k, (a, b) in enumerate(pairs)]
    for copy in copies:
        copy.start()
    for copy in copies:
        copy.wait()
    lane = lax.broadcasted_iota(jnp.int32, (1, BLOCK), 1)
    row = jnp.where(lane == codes.shape[0], count[0], 0)
    for p in range(codes.shape[0]):
        row = jnp.where(lane == p, codes[p], row)
    for f in range(SLABS):
        for a in range(3):
            out[f, 2 * a : 2 * a + 2, :] = field[f, a]
        out[f, 6:8, :] = pol[f]
        out[f, 8:16, :] = jnp.zeros((8, out.shape[2]), jnp.float32)
        out[f, 8:11, :] = pos[...]
        out[f, 11:12, 0:BLOCK] = row.astype(jnp.float32)


def join_kernel(got, applied, alpha, own, pos):
    for s in range(SLABS):
        for a in range(3):
            for i in range(2):
                row = 8 * a + 2 * s + i
                applied[row : row + 1, :] = got[s, 2 * a + i : 2 * a + i + 1, :]
        real, imag = got[s, 6:7, :], got[s, 7:8, :]
        alpha[2 * s : 2 * s + 1, :] = real
        alpha[2 * s + 1 : 2 * s + 2, :] = real
        alpha[8 + 2 * s : 9 + 2 * s, :] = -imag
        alpha[9 + 2 * s : 10 + 2 * s, :] = imag
        pos[3 * s : 3 * s + 3, :] = got[s, 8:11, :]
        own[24 + 3 * s : 27 + 3 * s, :] = got[s, 8:11, :]
        own[36 + s : 37 + s, :] = got[s, 11:12, :]
    for a in range(3):
        rows = slice(8 * a, 8 * a + 8)
        own[rows, :] = respond_rows(alpha[...], applied[rows, :])


def call(body, out_shape, scratch=(), in_specs=None, out_specs=None, aliases=None):
    specs = {} if in_specs is None else {"in_specs": in_specs, "out_specs": out_specs}
    return pl.pallas_call(
        body,
        out_shape=out_shape,
        **specs,
        scratch_shapes=list(scratch),
        input_output_aliases=aliases or {},
        compiler_params=pltpu.CompilerParams(vmem_limit_bytes=6 * 1024 * 1024),
    )


def shards(positions, polarizability, applied_field, pair_codes, pair_counts):
    rows = positions.shape[1]
    f32 = jnp.float32
    arr = lambda *shape: jax.ShapeDtypeStruct((*shape, rows), f32)
    held = lambda *shape: pltpu.VMEM((*shape, rows), f32)
    flip = lambda value: lax.ppermute(value, "gz", swaps(2, True))
    turn = lambda value, first: lax.ppermute(value, "gy", swaps(lax.axis_size("gy"), first))
    keep = lambda value: pltpu.with_memory_space_constraint(value, pltpu.VMEM)
    fixed = lambda value: pltpu.with_memory_space_constraint(value, pltpu.SMEM)
    arguments = (
        positions,
        polarizability,
        jnp.transpose(applied_field, (0, 2, 1, 3)),
        pair_codes,
    )
    sent = call(
        pack_kernel,
        arr(SLABS, 16),
        [pltpu.VMEM(value.shape, f32) for value in arguments[:3]]
        + [pltpu.SMEM(pair_codes.shape, jnp.int32), pltpu.SemaphoreType.DMA((4,))],
        [pl.BlockSpec(memory_space=pltpu.HBM)] * 4 + [SMEM],
        VMEM,
    )(*[pltpu.with_memory_space_constraint(value, pltpu.HBM) for value in arguments], pair_counts)
    got = lax.all_to_all(sent, "gx", 0, 0)
    applied, alpha, own, pos = call(join_kernel, (arr(24), arr(16), arr(40), arr(12)))(got)
    got = flip(own)
    pos_b = turn(pos, False)
    pos_a = turn(pos, True)
    tens_shape = pltpu.VMEM((KEPT, 2 * BLOCK, 6 * BLOCK), jnp.bfloat16)
    one = pltpu.VMEM((1, 2 * BLOCK, 6 * BLOCK), jnp.bfloat16)
    tgt_pos, acc = held(SLABS, 8), held(SLABS, 24)
    tens, tab, own_pos, got_pos = call(
        first_kernel,
        (tens_shape, pltpu.SMEM((12 * STRIDE,), jnp.int32), arr(SLABS, 8), arr(SLABS, 8)),
        (pltpu.SMEM((2 * SLABS, 1, BLOCK), f32), pltpu.SemaphoreType.DMA((2 * SLABS,))),
        [VMEM] * 2,
        (VMEM, SMEM, VMEM, VMEM),
    )(own, got)
    tab = fixed(tab)

    def first_far(slot, pos, tens):
        return call(
            functools.partial(first_far_kernel, slot),
            (arr(24), tens_shape),
            (tgt_pos, acc, one),
            [SMEM] + [VMEM] * 6,
            (VMEM, VMEM),
            {6: 1},
        )(tab, own, got, own_pos, got_pos, pos, keep(tens))

    def here(own, got):
        return call(here_kernel, arr(24), (acc, one), [SMEM] + [VMEM] * 5, VMEM)(
            tab, own, got, own_pos, got_pos, keep(tens)
        )

    def far(slot, got, pos, begun):
        return call(
            functools.partial(far_kernel, slot),
            arr(24),
            (tgt_pos, acc, one),
            [SMEM] + [VMEM] * 5,
            VMEM,
        )(tab, got, got_pos, pos, keep(tens), begun)

    msg, tens = first_far(2, pos_b, tens)
    from_b = turn(msg, False)
    msg, tens = first_far(1, pos_a, tens)
    from_a = turn(msg, True)
    field, tens = call(
        first_here_kernel,
        (arr(24), tens_shape),
        (acc, one),
        [SMEM] + [VMEM] * 5,
        (VMEM, VMEM),
        {5: 1},
    )(tab, own, got, own_pos, got_pos, keep(tens))
    for sweep in range(1, ITERS):
        own = call(update_kernel, arr(24))(field, from_a, from_b, applied, alpha)
        got = flip(own)
        at_a, at_b = call(
            own_kernel,
            (arr(SLABS, 24), arr(SLABS, 24)),
            (tgt_pos, one),
            [SMEM] + [VMEM] * 5,
            (VMEM, VMEM),
        )(tab, own, own_pos, pos_a, pos_b, keep(tens))
        from_b = turn(far(2, got, pos_b, at_b), False)
        from_a = turn(far(1, got, pos_a, at_a), True)
        field = here(own, got)
    out = call(last_kernel, arr(SLABS, 3, 2))(field, from_a, from_b, applied, alpha)
    return jnp.transpose(lax.all_to_all(out, "gx", 0, 0), (0, 2, 1, 3))


def solution(mesh):
    in_specs = (
        P(None, ("gx", "gy", "gz")),
        P(None, None, ("gx", "gy", "gz")),
        P(None, None, None, ("gx", "gy", "gz")),
        P(("gx", "gy", "gz")),
        P(("gx", "gy", "gz")),
    )
    out_specs = P(None, None, None, ("gx", "gy", "gz"))
    return jax.shard_map(shards, mesh=mesh, in_specs=in_specs, out_specs=out_specs, check_vma=False)
```

```python
import functools
import math

import jax
import jax.numpy as jnp
from jax import lax
from jax.experimental import pallas as pl
from jax.experimental.pallas import tpu as pltpu
from jax.sharding import PartitionSpec as P

BLOCK = 128
ITERS = 4

cell_width = 4.0
coupling = 0.8
root_pi = 1.0 / math.sqrt(math.pi)
erfcx_fit = (
    1.790011536,
    0.928601473,
    0.3238769782,
    0.05183749415,
    -0.01103335474,
    -0.006028563159,
    0.0006207049413,
    0.0006951546236,
    -6.044884693e-05,
    -6.930253734e-05,
)

VMEM = pl.BlockSpec(memory_space=pltpu.VMEM)
SMEM = pl.BlockSpec(memory_space=pltpu.SMEM)
SLABS = 4
KEPT = 72
STRIDE = 256


def swaps(count, first):
    if first:
        return [(i, i ^ 1) for i in range(count)]
    return [(i, (i + 1) % count if i % 2 else (i - 1) % count) for i in range(count)]


def columns(block):
    return pl.ds(pl.multiple_of(block * BLOCK, BLOCK), BLOCK)


def build(word, src_pos, tgt_pos, tens, slot):
    src_slab = (word >> 11) & 3
    tgt_slab = (word >> 16) & 3
    shift_x = (((word >> 18) & 3) - 1).astype(jnp.float32) * -cell_width
    shift_y = (((word >> 20) & 3) - 1).astype(jnp.float32) * cell_width
    tgt_cols = columns((word >> 13) & 7)
    tx, ty, tz = (tgt_pos[tgt_slab, k : k + 1, tgt_cols] for k in range(3))
    tx, ty = tx + shift_x, ty + shift_y
    source = jnp.transpose(src_pos[src_slab, :, columns((word >> 8) & 7)])
    chunk = 32
    for start in range(0, BLOCK, chunk):
        part = source[start : start + chunk]
        dx = tx - part[:, 0:1]
        dy = ty - part[:, 1:2]
        dz = tz - part[:, 2:3]
        dist_sq = dx * dx + dy * dy + dz * dz + 1.0
        inv_dist = lax.rsqrt(dist_sq)
        distance = dist_sq * inv_dist
        inv_sq = inv_dist * inv_dist
        reach = 1.0 / (distance + 4.0)
        at = reach * 10.0 - 1.0
        fit = jnp.full_like(at, erfcx_fit[-1])
        for coef in erfcx_fit[-2::-1]:
            fit = fit * at + coef
        decay = jnp.exp2(dist_sq * (-0.25 / math.log(2.0)))
        b_term = inv_sq * decay * (fit * reach * inv_dist + root_pi)
        c_term = inv_sq * (3.0 * b_term + (0.5 * root_pi) * decay)
        cx, cy, cz = c_term * dx, c_term * dy, c_term * dz
        comps = (cx * dx - b_term, cx * dy, cx * dz, cy * dy - b_term, cy * dz, cz * dz - b_term)
        for k, comp in enumerate(comps):
            high = comp.astype(jnp.bfloat16)
            low = (comp - high.astype(jnp.float32)).astype(jnp.bfloat16)
            cols = slice(k * BLOCK, (k + 1) * BLOCK)
            tens[slot, start : start + chunk, cols] = high
            tens[slot, BLOCK + start : BLOCK + start + chunk, cols] = low


def apply(words, slots, live, dip, tens, out):
    results = []
    row_slab = lax.broadcasted_iota(jnp.int32, (8, BLOCK), 0) // 2
    for word, slot, ok in zip(words, slots, live):
        src_slab = (word >> 11) & 3
        cols = columns((word >> 8) & 7)
        mine = row_slab == src_slab
        beside = row_slab == ((src_slab + 1) & 3)
        left, right = [], []
        for k in range(3):
            value = dip[8 * k : 8 * k + 8, cols]
            if ok is not None:
                value = jnp.where(ok, value, 0.0)
            high = value.astype(jnp.bfloat16).astype(jnp.float32)
            low = pltpu.roll(value - high, 2, 0)
            part = jnp.where(mine, high, 0.0)
            left.append(jnp.where(beside, low, part))
            right.append(part)
        lhs = jnp.concatenate(
            [jnp.concatenate(left, axis=0), jnp.concatenate(right, axis=0)], axis=1
        ).astype(jnp.bfloat16)
        results.append(
            lax.dot_general(
                lhs, tens[slot], (((1,), (0,)), ((), ())), preferred_element_type=jnp.float32
            )
        )
    pick = ((0, 1, 2), (1, 3, 4), (2, 4, 5))
    for word, res in zip(words, results):
        cols = columns((word >> 13) & 7)
        tgt_slab = (word >> 16) & 3
        for a in range(3):
            total = res[0:8, pick[a][0] * BLOCK : (pick[a][0] + 1) * BLOCK]
            for b in (1, 2):
                k = pick[a][b]
                total = total + res[8 * b : 8 * b + 8, k * BLOCK : (k + 1) * BLOCK]
            out[tgt_slab, 8 * a : 8 * a + 8, cols] += total


def each_build(tab, group, src_pos, tgt_pos, tens):
    base = group * STRIDE
    count = tab[base]

    def step(i, carry):
        for j in range(2):
            word = tab[base + 1 + jnp.minimum(2 * i + j, count - 1)]
            build(word, src_pos, tgt_pos, tens, word & 255)
        return carry

    lax.fori_loop(0, (count + 1) // 2, step, 0)


def each_apply(tab, group, dip, tens, out):
    base = group * STRIDE
    count = tab[base]

    def step(i, carry):
        words, live = [], []
        for j in range(4):
            at = 4 * i + j
            words.append(tab[base + 1 + jnp.minimum(at, count - 1)])
            live.append(None if j == 0 else at < count)
        apply(words, [word & 255 for word in words], live, dip, tens, out)
        return carry

    lax.fori_loop(0, (count + 3) // 4, step, 0)


def each_other(tab, group, src_pos, tgt_pos, dip, out, one):
    base = (group + 6) * STRIDE

    def step(i, carry):
        word = tab[base + 1 + i]
        build(word, src_pos, tgt_pos, one, 0)
        apply([word], [0], [None], dip, one, out)
        return carry

    lax.fori_loop(0, tab[base], step, 0)


def settle(acc, out):
    for a in range(3):
        rows = slice(8 * a, 8 * a + 8)
        joined = None
        for s in range(SLABS):
            part = acc[s, rows, :]
            part = part + pltpu.roll(part, 4, 0)
            part = part + pltpu.roll(part, 2, 0)
            mine = lax.broadcasted_iota(jnp.int32, part.shape, 0) // 2 == s
            joined = part if s == 0 else jnp.where(mine, part, joined)
        out[rows, :] = joined


def sort_entries(lists, tab):
    for group in range(12):
        tab[group * STRIDE] = 0
    core = lax.axis_index("gz")
    odd_y = lax.rem(lax.axis_index("gy"), 2)
    used = jnp.int32(0)
    for half in range(2):
        for slab in range(SLABS):
            which = half * SLABS + slab

            def place(p, used, half=half, slab=slab, which=which):
                code = lists[which, 0, p].astype(jnp.int32)
                steps = code >> 7
                step_x = (steps * 11) >> 5
                step_y = steps - 3 * step_x
                slot_y = jnp.where(step_y == 1, 0, jnp.where((step_y == 2) == (odd_y == 0), 1, 2))
                word = (
                    used
                    | ((code & 7) << 8)
                    | (((slab + step_x + SLABS - 1) & (SLABS - 1)) << 11)
                    | (((code >> 3) & 7) << 13)
                    | (slab << 16)
                    | (step_x << 18)
                    | (step_y << 20)
                )
                group = 3 * half + slot_y + jnp.where(used >= KEPT, 6, 0)
                hit = jnp.where(((code >> 6) & 1) == core, 1, 0)
                at = tab[group * STRIDE]
                tab[group * STRIDE + 1 + at] = word
                tab[group * STRIDE] = at + hit
                return used + hit

            used = lax.fori_loop(0, lists[which, 0, 24].astype(jnp.int32), place, used)


def spread(value, row, out):
    for s in range(SLABS):
        out[s, 0:3, :] = value[row + 3 * s : row + 3 * s + 3, :]


def first_kernel(own, got, tens, tab, own_pos, got_pos, lists, sems):
    copies = []
    for half, value in enumerate((own, got)):
        for s in range(SLABS):
            which = half * SLABS + s
            row = 36 + s
            copies.append(
                pltpu.make_async_copy(
                    value.at[row : row + 1, 0:BLOCK], lists.at[which], sems.at[which]
                )
            )
    for copy in copies:
        copy.start()
    own_pos[...] = jnp.zeros_like(own_pos)
    got_pos[...] = jnp.zeros_like(got_pos)
    spread(own, 24, own_pos)
    spread(got, 24, got_pos)
    for copy in copies:
        copy.wait()
    sort_entries(lists, tab)
    each_build(tab, 0, own_pos, own_pos, tens)


def first_far_kernel(slot, tab, own, got, own_pos, got_pos, pos, tens_in, out, tens, tgt_pos, acc, one):
    spread(pos, 0, tgt_pos)
    acc[...] = jnp.zeros_like(acc)
    for group, src_pos, dip in ((slot, own_pos, own), (3 + slot, got_pos, got)):
        each_build(tab, group, src_pos, tgt_pos, tens)
        each_apply(tab, group, dip, tens, acc)
        each_other(tab, group, src_pos, tgt_pos, dip, acc, one)
    settle(acc, out)


def own_kernel(tab, own, own_pos, pos_a, pos_b, tens, at_a, at_b, tgt_pos, one):
    for slot, pos, out in ((2, pos_b, at_b), (1, pos_a, at_a)):
        out[...] = jnp.zeros_like(out)
        each_apply(tab, slot, own, tens, out)
        spread(pos, 0, tgt_pos)
        each_other(tab, slot, own_pos, tgt_pos, own, out, one)


def far_kernel(slot, tab, got, got_pos, pos, tens, begun, out, tgt_pos, acc, one):
    acc[...] = begun[...]
    each_apply(tab, 3 + slot, got, tens, acc)
    spread(pos, 0, tgt_pos)
    each_other(tab, 3 + slot, got_pos, tgt_pos, got, acc, one)
    settle(acc, out)


def here_kernel(tab, own, got, own_pos, got_pos, tens, out, acc, one):
    acc[...] = jnp.zeros_like(acc)
    for group, src_pos, dip in ((0, own_pos, own), (3, got_pos, got)):
        each_apply(tab, group, dip, tens, acc)
        each_other(tab, group, src_pos, own_pos, dip, acc, one)
    settle(acc, out)


def first_here_kernel(tab, own, got, own_pos, got_pos, tens_in, out, tens, acc, one):
    each_build(tab, 3, got_pos, own_pos, tens)
    here_kernel(tab, own, got, own_pos, got_pos, tens, out, acc, one)


def respond_rows(alpha, total):
    real_row = lax.broadcasted_iota(jnp.int32, (8, total.shape[1]), 0) % 2 < 1
    turned = jnp.where(real_row, pltpu.roll(total, 7, 0), pltpu.roll(total, 1, 0))
    return alpha[0:8] * total + alpha[8:16] * turned


def update_kernel(field, from_a, from_b, applied, alpha, dip):
    for a in range(3):
        rows = slice(8 * a, 8 * a + 8)
        total = applied[rows, :] + coupling * (field[rows, :] + from_a[rows, :] + from_b[rows, :])
        dip[rows, :] = respond_rows(alpha[...], total)


def last_kernel(field, from_a, from_b, applied, alpha, out):
    for a in range(3):
        rows = slice(8 * a, 8 * a + 8)
        total = applied[rows, :] + coupling * (field[rows, :] + from_a[rows, :] + from_b[rows, :])
        dip = respond_rows(alpha[...], total)
        for s in range(SLABS):
            out[s, a] = dip[2 * s : 2 * s + 2]


def pack_kernel(pos_in, pol_in, field_in, codes_in, count, out, pos, pol, field, codes, sems):
    pairs = ((field_in, field), (pol_in, pol), (pos_in, pos), (codes_in, codes))
    copies = [pltpu.make_async_copy(a, b, sems.at[k]) for k, (a, b) in enumerate(pairs)]
    for copy in copies:
        copy.start()
    for copy in copies:
        copy.wait()
    lane = lax.broadcasted_iota(jnp.int32, (1, BLOCK), 1)
    row = jnp.where(lane == codes.shape[0], count[0], 0)
    for p in range(codes.shape[0]):
        row = jnp.where(lane == p, codes[p], row)
    for f in range(SLABS):
        out[f, 0, 0:2, :] = field[f, 0]
        out[f, 0, 2:4, :] = field[f, 1]
        out[f, 1, 0:2, :] = field[f, 2]
        out[f, 1, 2:4, :] = pol[f]
        out[f, 2, 0:3, :] = pos[...]
        out[f, 2, 3:4, :] = jnp.zeros((1, out.shape[3]), jnp.float32)
        out[f, 2, 3:4, 0:BLOCK] = row.astype(jnp.float32)


def join_kernel(got, applied, alpha, own, pos):
    for s in range(SLABS):
        for a in range(3):
            for i in range(2):
                row = 8 * a + 2 * s + i
                at = 2 * a + i
                applied[row : row + 1, :] = got[s, at // 4, at % 4 : at % 4 + 1, :]
        real, imag = got[s, 1, 2:3, :], got[s, 1, 3:4, :]
        alpha[2 * s : 2 * s + 1, :] = real
        alpha[2 * s + 1 : 2 * s + 2, :] = real
        alpha[8 + 2 * s : 9 + 2 * s, :] = -imag
        alpha[9 + 2 * s : 10 + 2 * s, :] = imag
        pos[3 * s : 3 * s + 3, :] = got[s, 2, 0:3, :]
        own[24 + 3 * s : 27 + 3 * s, :] = got[s, 2, 0:3, :]
        own[36 + s : 37 + s, :] = got[s, 2, 3:4, :]
    for a in range(3):
        rows = slice(8 * a, 8 * a + 8)
        own[rows, :] = respond_rows(alpha[...], applied[rows, :])


def call(body, out_shape, scratch=(), in_specs=None, out_specs=None, aliases=None):
    specs = {} if in_specs is None else {"in_specs": in_specs, "out_specs": out_specs}
    return pl.pallas_call(
        body,
        out_shape=out_shape,
        **specs,
        scratch_shapes=list(scratch),
        input_output_aliases=aliases or {},
        compiler_params=pltpu.CompilerParams(vmem_limit_bytes=6 * 1024 * 1024),
    )


def shards(positions, polarizability, applied_field, pair_codes, pair_counts):
    rows = positions.shape[1]
    f32 = jnp.float32
    arr = lambda *shape: jax.ShapeDtypeStruct((*shape, rows), f32)
    held = lambda *shape: pltpu.VMEM((*shape, rows), f32)
    flip = lambda value: lax.ppermute(value, "gz", swaps(2, True))
    turn = lambda value, first: lax.ppermute(value, "gy", swaps(lax.axis_size("gy"), first))
    keep = lambda value: pltpu.with_memory_space_constraint(value, pltpu.VMEM)
    fixed = lambda value: pltpu.with_memory_space_constraint(value, pltpu.SMEM)
    arguments = (
        positions,
        polarizability,
        jnp.transpose(applied_field, (0, 2, 1, 3)),
        pair_codes,
    )
    sent = call(
        pack_kernel,
        arr(SLABS, 3, 4),
        [pltpu.VMEM(value.shape, f32) for value in arguments[:3]]
        + [pltpu.SMEM(pair_codes.shape, jnp.int32), pltpu.SemaphoreType.DMA((4,))],
        [pl.BlockSpec(memory_space=pltpu.HBM)] * 4 + [SMEM],
        VMEM,
    )(*[pltpu.with_memory_space_constraint(value, pltpu.HBM) for value in arguments], pair_counts)
    got = lax.all_to_all(sent, "gx", 0, 0)
    applied, alpha, own, pos = call(join_kernel, (arr(24), arr(16), arr(40), arr(12)))(got)
    got = flip(own)
    pos_b = turn(pos, False)
    pos_a = turn(pos, True)
    tens_shape = pltpu.VMEM((KEPT, 2 * BLOCK, 6 * BLOCK), jnp.bfloat16)
    one = pltpu.VMEM((1, 2 * BLOCK, 6 * BLOCK), jnp.bfloat16)
    tgt_pos, acc = held(SLABS, 8), held(SLABS, 24)
    tens, tab, own_pos, got_pos = call(
        first_kernel,
        (tens_shape, pltpu.SMEM((12 * STRIDE,), jnp.int32), arr(SLABS, 8), arr(SLABS, 8)),
        (pltpu.SMEM((2 * SLABS, 1, BLOCK), f32), pltpu.SemaphoreType.DMA((2 * SLABS,))),
        [VMEM] * 2,
        (VMEM, SMEM, VMEM, VMEM),
    )(own, got)
    tab = fixed(tab)

    def first_far(slot, pos, tens):
        return call(
            functools.partial(first_far_kernel, slot),
            (arr(24), tens_shape),
            (tgt_pos, acc, one),
            [SMEM] + [VMEM] * 6,
            (VMEM, VMEM),
            {6: 1},
        )(tab, own, got, own_pos, got_pos, pos, keep(tens))

    def here(own, got):
        return call(here_kernel, arr(24), (acc, one), [SMEM] + [VMEM] * 5, VMEM)(
            tab, own, got, own_pos, got_pos, keep(tens)
        )

    def far(slot, got, pos, begun):
        return call(
            functools.partial(far_kernel, slot),
            arr(24),
            (tgt_pos, acc, one),
            [SMEM] + [VMEM] * 5,
            VMEM,
        )(tab, got, got_pos, pos, keep(tens), begun)

    msg_a, tens = first_far(1, pos_a, tens)
    msg_b, tens = first_far(2, pos_b, tens)
    from_b = turn(msg_b, False)
    from_a = turn(msg_a, True)
    field, tens = call(
        first_here_kernel,
        (arr(24), tens_shape),
        (acc, one),
        [SMEM] + [VMEM] * 5,
        (VMEM, VMEM),
        {5: 1},
    )(tab, own, got, own_pos, got_pos, keep(tens))
    for sweep in range(1, ITERS):
        own = call(update_kernel, arr(24))(field, from_a, from_b, applied, alpha)
        got = flip(own)
        at_a, at_b = call(
            own_kernel,
            (arr(SLABS, 24), arr(SLABS, 24)),
            (tgt_pos, one),
            [SMEM] + [VMEM] * 5,
            (VMEM, VMEM),
        )(tab, own, own_pos, pos_a, pos_b, keep(tens))
        from_b = turn(far(2, got, pos_b, at_b), False)
        from_a = turn(far(1, got, pos_a, at_a), True)
        field = here(own, got)
    out = call(last_kernel, arr(SLABS, 3, 2))(field, from_a, from_b, applied, alpha)
    return jnp.transpose(lax.all_to_all(out, "gx", 0, 0), (0, 2, 1, 3))


def solution(mesh):
    in_specs = (
        P(None, ("gx", "gy", "gz")),
        P(None, None, ("gx", "gy", "gz")),
        P(None, None, None, ("gx", "gy", "gz")),
        P(("gx", "gy", "gz")),
        P(("gx", "gy", "gz")),
    )
    out_specs = P(None, None, None, ("gx", "gy", "gz"))
    return jax.shard_map(shards, mesh=mesh, in_specs=in_specs, out_specs=out_specs, check_vma=False)
```

```python
import functools
import math

import jax
import jax.numpy as jnp
from jax import lax
from jax.experimental import pallas as pl
from jax.experimental.pallas import tpu as pltpu
from jax.sharding import PartitionSpec as P

BLOCK = 128
ITERS = 4

cell_width = 4.0
coupling = 0.8
root_pi = 1.0 / math.sqrt(math.pi)
erfcx_fit = (
    1.790011536,
    0.928601473,
    0.3238769782,
    0.05183749415,
    -0.01103335474,
    -0.006028563159,
    0.0006207049413,
    0.0006951546236,
    -6.044884693e-05,
    -6.930253734e-05,
)

VMEM = pl.BlockSpec(memory_space=pltpu.VMEM)
SMEM = pl.BlockSpec(memory_space=pltpu.SMEM)
SLABS = 4
KEPT = 72
STRIDE = 256


def swaps(count, first):
    if first:
        return [(i, i ^ 1) for i in range(count)]
    return [(i, (i + 1) % count if i % 2 else (i - 1) % count) for i in range(count)]


def columns(block):
    return pl.ds(pl.multiple_of(block * BLOCK, BLOCK), BLOCK)


def build(word, src_pos, tgt_pos, tens, slot):
    src_slab = (word >> 11) & 3
    tgt_slab = (word >> 16) & 3
    shift_x = (((word >> 18) & 3) - 1).astype(jnp.float32) * -cell_width
    shift_y = (((word >> 20) & 3) - 1).astype(jnp.float32) * cell_width
    tgt_cols = columns((word >> 13) & 7)
    tx, ty, tz = (tgt_pos[tgt_slab, k : k + 1, tgt_cols] for k in range(3))
    tx, ty = tx + shift_x, ty + shift_y
    source = jnp.transpose(src_pos[src_slab, :, columns((word >> 8) & 7)])
    chunk = 32
    for start in range(0, BLOCK, chunk):
        part = source[start : start + chunk]
        dx = tx - part[:, 0:1]
        dy = ty - part[:, 1:2]
        dz = tz - part[:, 2:3]
        dist_sq = dx * dx + dy * dy + dz * dz + 1.0
        inv_dist = lax.rsqrt(dist_sq)
        distance = dist_sq * inv_dist
        inv_sq = inv_dist * inv_dist
        reach = 1.0 / (distance + 4.0)
        at = reach * 10.0 - 1.0
        fit = jnp.full_like(at, erfcx_fit[-1])
        for coef in erfcx_fit[-2::-1]:
            fit = fit * at + coef
        decay = jnp.exp2(dist_sq * (-0.25 / math.log(2.0)))
        b_term = inv_sq * decay * (fit * reach * inv_dist + root_pi)
        c_term = inv_sq * (3.0 * b_term + (0.5 * root_pi) * decay)
        cx, cy, cz = c_term * dx, c_term * dy, c_term * dz
        comps = (cx * dx - b_term, cx * dy, cx * dz, cy * dy - b_term, cy * dz, cz * dz - b_term)
        for k, comp in enumerate(comps):
            high = comp.astype(jnp.bfloat16)
            low = (comp - high.astype(jnp.float32)).astype(jnp.bfloat16)
            cols = slice(k * BLOCK, (k + 1) * BLOCK)
            tens[slot, start : start + chunk, cols] = high
            tens[slot, BLOCK + start : BLOCK + start + chunk, cols] = low


def apply(words, slots, live, dip, tens, out):
    results = []
    row_slab = lax.broadcasted_iota(jnp.int32, (8, BLOCK), 0) // 2
    for word, slot, ok in zip(words, slots, live):
        src_slab = (word >> 11) & 3
        cols = columns((word >> 8) & 7)
        mine = row_slab == src_slab
        beside = row_slab == ((src_slab + 1) & 3)
        left, right = [], []
        for k in range(3):
            value = dip[8 * k : 8 * k + 8, cols]
            if ok is not None:
                value = jnp.where(ok, value, 0.0)
            high = value.astype(jnp.bfloat16).astype(jnp.float32)
            low = pltpu.roll(value - high, 2, 0)
            part = jnp.where(mine, high, 0.0)
            left.append(jnp.where(beside, low, part))
            right.append(part)
        lhs = jnp.concatenate(
            [jnp.concatenate(left, axis=0), jnp.concatenate(right, axis=0)], axis=1
        ).astype(jnp.bfloat16)
        results.append(
            lax.dot_general(
                lhs, tens[slot], (((1,), (0,)), ((), ())), preferred_element_type=jnp.float32
            )
        )
    pick = ((0, 1, 2), (1, 3, 4), (2, 4, 5))
    for word, res in zip(words, results):
        cols = columns((word >> 13) & 7)
        tgt_slab = (word >> 16) & 3
        for a in range(3):
            total = res[0:8, pick[a][0] * BLOCK : (pick[a][0] + 1) * BLOCK]
            for b in (1, 2):
                k = pick[a][b]
                total = total + res[8 * b : 8 * b + 8, k * BLOCK : (k + 1) * BLOCK]
            out[tgt_slab, 8 * a : 8 * a + 8, cols] += total


def each_build(tab, group, src_pos, tgt_pos, tens):
    base = group * STRIDE
    count = tab[base]

    def step(i, carry):
        for j in range(2):
            word = tab[base + 1 + jnp.minimum(2 * i + j, count - 1)]
            build(word, src_pos, tgt_pos, tens, word & 255)
        return carry

    lax.fori_loop(0, (count + 1) // 2, step, 0)


def each_apply(tab, group, dip, tens, out):
    base = group * STRIDE
    count = tab[base]

    def step(i, carry):
        words, live = [], []
        for j in range(4):
            at = 4 * i + j
            words.append(tab[base + 1 + jnp.minimum(at, count - 1)])
            live.append(None if j == 0 else at < count)
        apply(words, [word & 255 for word in words], live, dip, tens, out)
        return carry

    lax.fori_loop(0, (count + 3) // 4, step, 0)


def each_other(tab, group, src_pos, tgt_pos, dip, out, one):
    base = (group + 6) * STRIDE

    def step(i, carry):
        word = tab[base + 1 + i]
        build(word, src_pos, tgt_pos, one, 0)
        apply([word], [0], [None], dip, one, out)
        return carry

    lax.fori_loop(0, tab[base], step, 0)


def settle(acc, out):
    for a in range(3):
        rows = slice(8 * a, 8 * a + 8)
        joined = None
        for s in range(SLABS):
            part = acc[s, rows, :]
            part = part + pltpu.roll(part, 4, 0)
            part = part + pltpu.roll(part, 2, 0)
            mine = lax.broadcasted_iota(jnp.int32, part.shape, 0) // 2 == s
            joined = part if s == 0 else jnp.where(mine, part, joined)
        out[rows, :] = joined


def sort_entries(lists, tab):
    for group in range(12):
        tab[group * STRIDE] = 0
    core = lax.axis_index("gz")
    odd_y = lax.rem(lax.axis_index("gy"), 2)
    used = jnp.int32(0)
    for half in range(2):
        for slab in range(SLABS):
            which = half * SLABS + slab

            def place(p, used, half=half, slab=slab, which=which):
                code = lists[which, 0, p].astype(jnp.int32)
                hit = ((code >> 6) & 1) == core

                @pl.when(hit)
                def _():
                    steps = code >> 7
                    step_x = (steps * 11) >> 5
                    step_y = steps - 3 * step_x
                    slot_y = jnp.where(
                        step_y == 1, 0, jnp.where((step_y == 2) == (odd_y == 0), 1, 2)
                    )
                    word = (
                        used
                        | ((code & 7) << 8)
                        | (((slab + step_x + SLABS - 1) & (SLABS - 1)) << 11)
                        | (((code >> 3) & 7) << 13)
                        | (slab << 16)
                        | (step_x << 18)
                        | (step_y << 20)
                    )
                    head = (3 * half + slot_y + jnp.where(used >= KEPT, 6, 0)) * STRIDE
                    count = tab[head] + 1
                    tab[head + count] = word
                    tab[head] = count

                return used + jnp.where(hit, 1, 0)

            used = lax.fori_loop(0, lists[which, 0, 24].astype(jnp.int32), place, used)


def spread(value, row, out):
    for s in range(SLABS):
        out[s, 0:3, :] = value[row + 3 * s : row + 3 * s + 3, :]


def first_kernel(own, got, tens, tab, own_pos, got_pos, lists, sems):
    copies = []
    for half, value in enumerate((own, got)):
        for s in range(SLABS):
            which = half * SLABS + s
            row = 36 + s
            copies.append(
                pltpu.make_async_copy(
                    value.at[row : row + 1, 0:BLOCK], lists.at[which], sems.at[which]
                )
            )
    for copy in copies:
        copy.start()
    own_pos[...] = jnp.zeros_like(own_pos)
    got_pos[...] = jnp.zeros_like(got_pos)
    spread(own, 24, own_pos)
    spread(got, 24, got_pos)
    for copy in copies:
        copy.wait()
    sort_entries(lists, tab)
    each_build(tab, 0, own_pos, own_pos, tens)


def first_far_kernel(slot, tab, own, got, own_pos, got_pos, pos, tens_in, out, tens, tgt_pos, acc, one):
    spread(pos, 0, tgt_pos)
    acc[...] = jnp.zeros_like(acc)
    for group, src_pos, dip in ((slot, own_pos, own), (3 + slot, got_pos, got)):
        each_build(tab, group, src_pos, tgt_pos, tens)
        each_apply(tab, group, dip, tens, acc)
        each_other(tab, group, src_pos, tgt_pos, dip, acc, one)
    settle(acc, out)


def own_kernel(tab, own, own_pos, pos_a, pos_b, tens, at_a, at_b, tgt_pos, one):
    for slot, pos, out in ((2, pos_b, at_b), (1, pos_a, at_a)):
        out[...] = jnp.zeros_like(out)
        each_apply(tab, slot, own, tens, out)
        spread(pos, 0, tgt_pos)
        each_other(tab, slot, own_pos, tgt_pos, own, out, one)


def far_kernel(slot, tab, got, got_pos, pos, tens, begun, out, tgt_pos, acc, one):
    acc[...] = begun[...]
    each_apply(tab, 3 + slot, got, tens, acc)
    spread(pos, 0, tgt_pos)
    each_other(tab, 3 + slot, got_pos, tgt_pos, got, acc, one)
    settle(acc, out)


def here_kernel(tab, own, got, own_pos, got_pos, tens, out, acc, one):
    acc[...] = jnp.zeros_like(acc)
    for group, src_pos, dip in ((0, own_pos, own), (3, got_pos, got)):
        each_apply(tab, group, dip, tens, acc)
        each_other(tab, group, src_pos, own_pos, dip, acc, one)
    settle(acc, out)


def first_here_kernel(tab, own, got, own_pos, got_pos, tens_in, out, tens, acc, one):
    each_build(tab, 3, got_pos, own_pos, tens)
    here_kernel(tab, own, got, own_pos, got_pos, tens, out, acc, one)


def respond_rows(alpha, total):
    real_row = lax.broadcasted_iota(jnp.int32, (8, total.shape[1]), 0) % 2 < 1
    turned = jnp.where(real_row, pltpu.roll(total, 7, 0), pltpu.roll(total, 1, 0))
    return alpha[0:8] * total + alpha[8:16] * turned


def update_kernel(field, from_a, from_b, applied, alpha, dip):
    for a in range(3):
        rows = slice(8 * a, 8 * a + 8)
        total = applied[rows, :] + coupling * (field[rows, :] + from_a[rows, :] + from_b[rows, :])
        dip[rows, :] = respond_rows(alpha[...], total)


def last_kernel(field, from_a, from_b, applied, alpha, out):
    for a in range(3):
        rows = slice(8 * a, 8 * a + 8)
        total = applied[rows, :] + coupling * (field[rows, :] + from_a[rows, :] + from_b[rows, :])
        dip = respond_rows(alpha[...], total)
        for s in range(SLABS):
            out[s, a] = dip[2 * s : 2 * s + 2]


def pack_kernel(pos_in, pol_in, field_in, codes_in, count, out, pos, pol, field, codes, sems):
    pairs = ((field_in, field), (pol_in, pol), (pos_in, pos), (codes_in, codes))
    copies = [pltpu.make_async_copy(a, b, sems.at[k]) for k, (a, b) in enumerate(pairs)]
    for copy in copies:
        copy.start()
    for copy in copies:
        copy.wait()
    lane = lax.broadcasted_iota(jnp.int32, (1, BLOCK), 1)
    row = jnp.where(lane == codes.shape[0], count[0], 0)
    for p in range(codes.shape[0]):
        row = jnp.where(lane == p, codes[p], row)
    for f in range(SLABS):
        out[f, 0, 0:2, :] = field[f, 0]
        out[f, 0, 2:4, :] = field[f, 1]
        out[f, 1, 0:2, :] = field[f, 2]
        out[f, 1, 2:4, :] = pol[f]
        out[f, 2, 0:3, :] = pos[...]
        out[f, 2, 3:4, :] = jnp.zeros((1, out.shape[3]), jnp.float32)
        out[f, 2, 3:4, 0:BLOCK] = row.astype(jnp.float32)


def join_kernel(got, applied, alpha, own, pos):
    for s in range(SLABS):
        for a in range(3):
            for i in range(2):
                row = 8 * a + 2 * s + i
                at = 2 * a + i
                applied[row : row + 1, :] = got[s, at // 4, at % 4 : at % 4 + 1, :]
        real, imag = got[s, 1, 2:3, :], got[s, 1, 3:4, :]
        alpha[2 * s : 2 * s + 1, :] = real
        alpha[2 * s + 1 : 2 * s + 2, :] = real
        alpha[8 + 2 * s : 9 + 2 * s, :] = -imag
        alpha[9 + 2 * s : 10 + 2 * s, :] = imag
        pos[3 * s : 3 * s + 3, :] = got[s, 2, 0:3, :]
        own[24 + 3 * s : 27 + 3 * s, :] = got[s, 2, 0:3, :]
        own[36 + s : 37 + s, :] = got[s, 2, 3:4, :]
    for a in range(3):
        rows = slice(8 * a, 8 * a + 8)
        own[rows, :] = respond_rows(alpha[...], applied[rows, :])


def call(body, out_shape, scratch=(), in_specs=None, out_specs=None, aliases=None):
    specs = {} if in_specs is None else {"in_specs": in_specs, "out_specs": out_specs}
    return pl.pallas_call(
        body,
        out_shape=out_shape,
        **specs,
        scratch_shapes=list(scratch),
        input_output_aliases=aliases or {},
        compiler_params=pltpu.CompilerParams(vmem_limit_bytes=6 * 1024 * 1024),
    )


def shards(positions, polarizability, applied_field, pair_codes, pair_counts):
    rows = positions.shape[1]
    f32 = jnp.float32
    arr = lambda *shape: jax.ShapeDtypeStruct((*shape, rows), f32)
    held = lambda *shape: pltpu.VMEM((*shape, rows), f32)
    flip = lambda value: lax.ppermute(value, "gz", swaps(2, True))
    turn = lambda value, first: lax.ppermute(value, "gy", swaps(lax.axis_size("gy"), first))
    keep = lambda value: pltpu.with_memory_space_constraint(value, pltpu.VMEM)
    fixed = lambda value: pltpu.with_memory_space_constraint(value, pltpu.SMEM)
    arguments = (
        positions,
        polarizability,
        jnp.transpose(applied_field, (0, 2, 1, 3)),
        pair_codes,
    )
    sent = call(
        pack_kernel,
        arr(SLABS, 3, 4),
        [pltpu.VMEM(value.shape, f32) for value in arguments[:3]]
        + [pltpu.SMEM(pair_codes.shape, jnp.int32), pltpu.SemaphoreType.DMA((4,))],
        [pl.BlockSpec(memory_space=pltpu.HBM)] * 4 + [SMEM],
        VMEM,
    )(*[pltpu.with_memory_space_constraint(value, pltpu.HBM) for value in arguments], pair_counts)
    got = lax.all_to_all(sent, "gx", 0, 0)
    applied, alpha, own, pos = call(join_kernel, (arr(24), arr(16), arr(40), arr(12)))(got)
    got = flip(own)
    pos_b = turn(pos, False)
    pos_a = turn(pos, True)
    tens_shape = pltpu.VMEM((KEPT, 2 * BLOCK, 6 * BLOCK), jnp.bfloat16)
    one = pltpu.VMEM((1, 2 * BLOCK, 6 * BLOCK), jnp.bfloat16)
    tgt_pos, acc = held(SLABS, 8), held(SLABS, 24)
    tens, tab, own_pos, got_pos = call(
        first_kernel,
        (tens_shape, pltpu.SMEM((12 * STRIDE,), jnp.int32), arr(SLABS, 8), arr(SLABS, 8)),
        (pltpu.SMEM((2 * SLABS, 1, BLOCK), f32), pltpu.SemaphoreType.DMA((2 * SLABS,))),
        [VMEM] * 2,
        (VMEM, SMEM, VMEM, VMEM),
    )(own, got)
    tab = fixed(tab)

    def first_far(slot, pos, tens):
        return call(
            functools.partial(first_far_kernel, slot),
            (arr(24), tens_shape),
            (tgt_pos, acc, one),
            [SMEM] + [VMEM] * 6,
            (VMEM, VMEM),
            {6: 1},
        )(tab, own, got, own_pos, got_pos, pos, keep(tens))

    def here(own, got):
        return call(here_kernel, arr(24), (acc, one), [SMEM] + [VMEM] * 5, VMEM)(
            tab, own, got, own_pos, got_pos, keep(tens)
        )

    def far(slot, got, pos, begun):
        return call(
            functools.partial(far_kernel, slot),
            arr(24),
            (tgt_pos, acc, one),
            [SMEM] + [VMEM] * 5,
            VMEM,
        )(tab, got, got_pos, pos, keep(tens), begun)

    msg_a, tens = first_far(1, pos_a, tens)
    msg_b, tens = first_far(2, pos_b, tens)
    from_b = turn(msg_b, False)
    from_a = turn(msg_a, True)
    field, tens = call(
        first_here_kernel,
        (arr(24), tens_shape),
        (acc, one),
        [SMEM] + [VMEM] * 5,
        (VMEM, VMEM),
        {5: 1},
    )(tab, own, got, own_pos, got_pos, keep(tens))
    for sweep in range(1, ITERS):
        own = call(update_kernel, arr(24))(field, from_a, from_b, applied, alpha)
        got = flip(own)
        at_a, at_b = call(
            own_kernel,
            (arr(SLABS, 24), arr(SLABS, 24)),
            (tgt_pos, one),
            [SMEM] + [VMEM] * 5,
            (VMEM, VMEM),
        )(tab, own, own_pos, pos_a, pos_b, keep(tens))
        from_b = turn(far(2, got, pos_b, at_b), False)
        from_a = turn(far(1, got, pos_a, at_a), True)
        field = here(own, got)
    out = call(last_kernel, arr(SLABS, 3, 2))(field, from_a, from_b, applied, alpha)
    return jnp.transpose(lax.all_to_all(out, "gx", 0, 0), (0, 2, 1, 3))


def solution(mesh):
    in_specs = (
        P(None, ("gx", "gy", "gz")),
        P(None, None, ("gx", "gy", "gz")),
        P(None, None, None, ("gx", "gy", "gz")),
        P(("gx", "gy", "gz")),
        P(("gx", "gy", "gz")),
    )
    out_specs = P(None, None, None, ("gx", "gy", "gz"))
    return jax.shard_map(shards, mesh=mesh, in_specs=in_specs, out_specs=out_specs, check_vma=False)
```

```python
import functools
import math

import jax
import jax.numpy as jnp
from jax import lax
from jax.experimental import pallas as pl
from jax.experimental.pallas import tpu as pltpu
from jax.sharding import PartitionSpec as P

BLOCK = 128
ITERS = 4

cell_width = 4.0
coupling = 0.8
root_pi = 1.0 / math.sqrt(math.pi)
erfcx_fit = (
    1.790011536,
    0.928601473,
    0.3238769782,
    0.05183749415,
    -0.01103335474,
    -0.006028563159,
    0.0006207049413,
    0.0006951546236,
    -6.044884693e-05,
    -6.930253734e-05,
)

VMEM = pl.BlockSpec(memory_space=pltpu.VMEM)
SMEM = pl.BlockSpec(memory_space=pltpu.SMEM)
SLABS = 4
KEPT = 72
STRIDE = 256


def swaps(count, first):
    if first:
        return [(i, i ^ 1) for i in range(count)]
    return [(i, (i + 1) % count if i % 2 else (i - 1) % count) for i in range(count)]


def columns(block):
    return pl.ds(pl.multiple_of(block * BLOCK, BLOCK), BLOCK)


def build(word, src_pos, tgt_pos, tens, slot):
    src_slab = (word >> 11) & 3
    tgt_slab = (word >> 16) & 3
    shift_x = (((word >> 18) & 3) - 1).astype(jnp.float32) * -cell_width
    shift_y = (((word >> 20) & 3) - 1).astype(jnp.float32) * cell_width
    tgt_cols = columns((word >> 13) & 7)
    tx, ty, tz = (tgt_pos[tgt_slab, k : k + 1, tgt_cols] for k in range(3))
    tx, ty = tx + shift_x, ty + shift_y
    source = jnp.transpose(src_pos[src_slab, :, columns((word >> 8) & 7)])
    chunk = 32
    for start in range(0, BLOCK, chunk):
        part = source[start : start + chunk]
        dx = tx - part[:, 0:1]
        dy = ty - part[:, 1:2]
        dz = tz - part[:, 2:3]
        dist_sq = dx * dx + dy * dy + dz * dz + 1.0
        inv_dist = lax.rsqrt(dist_sq)
        distance = dist_sq * inv_dist
        inv_sq = inv_dist * inv_dist
        reach = 1.0 / (distance + 4.0)
        at = reach * 10.0 - 1.0
        fit = jnp.full_like(at, erfcx_fit[-1])
        for coef in erfcx_fit[-2::-1]:
            fit = fit * at + coef
        decay = jnp.exp2(dist_sq * (-0.25 / math.log(2.0)))
        b_term = inv_sq * decay * (fit * reach * inv_dist + root_pi)
        c_term = inv_sq * (3.0 * b_term + (0.5 * root_pi) * decay)
        cx, cy, cz = c_term * dx, c_term * dy, c_term * dz
        comps = (cx * dx - b_term, cx * dy, cx * dz, cy * dy - b_term, cy * dz, cz * dz - b_term)
        for k, comp in enumerate(comps):
            high = comp.astype(jnp.bfloat16)
            low = (comp - high.astype(jnp.float32)).astype(jnp.bfloat16)
            cols = slice(k * BLOCK, (k + 1) * BLOCK)
            tens[slot, start : start + chunk, cols] = high
            tens[slot, BLOCK + start : BLOCK + start + chunk, cols] = low


def apply(words, slots, live, dip, tens, out):
    results = []
    row_slab = lax.broadcasted_iota(jnp.int32, (8, BLOCK), 0) // 2
    for word, slot, ok in zip(words, slots, live):
        src_slab = (word >> 11) & 3
        cols = columns((word >> 8) & 7)
        mine = row_slab == src_slab
        beside = row_slab == ((src_slab + 1) & 3)
        left, right = [], []
        for k in range(3):
            value = dip[8 * k : 8 * k + 8, cols]
            if ok is not None:
                value = jnp.where(ok, value, 0.0)
            high = value.astype(jnp.bfloat16).astype(jnp.float32)
            low = pltpu.roll(value - high, 2, 0)
            part = jnp.where(mine, high, 0.0)
            left.append(jnp.where(beside, low, part))
            right.append(part)
        lhs = jnp.concatenate(
            [jnp.concatenate(left, axis=0), jnp.concatenate(right, axis=0)], axis=1
        ).astype(jnp.bfloat16)
        results.append(
            lax.dot_general(
                lhs, tens[slot], (((1,), (0,)), ((), ())), preferred_element_type=jnp.float32
            )
        )
    pick = ((0, 1, 2), (1, 3, 4), (2, 4, 5))
    for word, res in zip(words, results):
        cols = columns((word >> 13) & 7)
        tgt_slab = (word >> 16) & 3
        for a in range(3):
            total = res[0:8, pick[a][0] * BLOCK : (pick[a][0] + 1) * BLOCK]
            for b in (1, 2):
                k = pick[a][b]
                total = total + res[8 * b : 8 * b + 8, k * BLOCK : (k + 1) * BLOCK]
            out[tgt_slab, 8 * a : 8 * a + 8, cols] += total


def each_build(tab, group, src_pos, tgt_pos, tens):
    base = group * STRIDE
    count = tab[base]

    def step(i, carry):
        for j in range(3):
            word = tab[base + 1 + jnp.minimum(3 * i + j, count - 1)]
            build(word, src_pos, tgt_pos, tens, word & 255)
        return carry

    lax.fori_loop(0, (count + 2) // 3, step, 0)


def each_apply(tab, group, dip, tens, out):
    base = group * STRIDE
    count = tab[base]

    def step(i, carry):
        words, live = [], []
        for j in range(4):
            at = 4 * i + j
            words.append(tab[base + 1 + jnp.minimum(at, count - 1)])
            live.append(None if j == 0 else at < count)
        apply(words, [word & 255 for word in words], live, dip, tens, out)
        return carry

    lax.fori_loop(0, (count + 3) // 4, step, 0)


def each_other(tab, group, src_pos, tgt_pos, dip, out, one):
    base = (group + 6) * STRIDE

    def step(i, carry):
        word = tab[base + 1 + i]
        build(word, src_pos, tgt_pos, one, 0)
        apply([word], [0], [None], dip, one, out)
        return carry

    lax.fori_loop(0, tab[base], step, 0)


def settle(acc, out):
    for a in range(3):
        rows = slice(8 * a, 8 * a + 8)
        joined = None
        for s in range(SLABS):
            part = acc[s, rows, :]
            part = part + pltpu.roll(part, 4, 0)
            part = part + pltpu.roll(part, 2, 0)
            mine = lax.broadcasted_iota(jnp.int32, part.shape, 0) // 2 == s
            joined = part if s == 0 else jnp.where(mine, part, joined)
        out[rows, :] = joined


def sort_entries(lists, tab):
    for group in range(12):
        tab[group * STRIDE] = 0
    core = lax.axis_index("gz")
    odd_y = lax.rem(lax.axis_index("gy"), 2)
    used = jnp.int32(0)
    for half in range(2):
        for slab in range(SLABS):
            which = half * SLABS + slab

            def place(p, used, half=half, slab=slab, which=which):
                code = lists[which, 0, p].astype(jnp.int32)
                steps = code >> 7
                step_x = (steps * 11) >> 5
                step_y = steps - 3 * step_x
                slot_y = jnp.where(step_y == 1, 0, jnp.where((step_y == 2) == (odd_y == 0), 1, 2))
                word = (
                    used
                    | ((code & 7) << 8)
                    | (((slab + step_x + SLABS - 1) & (SLABS - 1)) << 11)
                    | (((code >> 3) & 7) << 13)
                    | (slab << 16)
                    | (step_x << 18)
                    | (step_y << 20)
                )
                group = 3 * half + slot_y + jnp.where(used >= KEPT, 6, 0)
                hit = jnp.where(((code >> 6) & 1) == core, 1, 0)
                at = tab[group * STRIDE]
                tab[group * STRIDE + 1 + at] = word
                tab[group * STRIDE] = at + hit
                return used + hit

            used = lax.fori_loop(0, lists[which, 0, 24].astype(jnp.int32), place, used)


def spread(value, row, out):
    for s in range(SLABS):
        out[s, 0:3, :] = value[row + 3 * s : row + 3 * s + 3, :]


def first_kernel(own, got, tens, tab, own_pos, got_pos, lists, sems):
    copies = []
    for half, value in enumerate((own, got)):
        for s in range(SLABS):
            which = half * SLABS + s
            row = 36 + s
            copies.append(
                pltpu.make_async_copy(
                    value.at[row : row + 1, 0:BLOCK], lists.at[which], sems.at[which]
                )
            )
    for copy in copies:
        copy.start()
    own_pos[...] = jnp.zeros_like(own_pos)
    got_pos[...] = jnp.zeros_like(got_pos)
    spread(own, 24, own_pos)
    spread(got, 24, got_pos)
    for copy in copies:
        copy.wait()
    sort_entries(lists, tab)
    each_build(tab, 0, own_pos, own_pos, tens)


def first_far_kernel(slot, tab, own, got, own_pos, got_pos, pos, tens_in, out, tens, tgt_pos, acc, one):
    spread(pos, 0, tgt_pos)
    acc[...] = jnp.zeros_like(acc)
    for group, src_pos, dip in ((slot, own_pos, own), (3 + slot, got_pos, got)):
        each_build(tab, group, src_pos, tgt_pos, tens)
        each_apply(tab, group, dip, tens, acc)
        each_other(tab, group, src_pos, tgt_pos, dip, acc, one)
    settle(acc, out)


def own_kernel(tab, own, own_pos, pos_a, pos_b, tens, at_a, at_b, tgt_pos, one):
    for slot, pos, out in ((2, pos_b, at_b), (1, pos_a, at_a)):
        out[...] = jnp.zeros_like(out)
        each_apply(tab, slot, own, tens, out)
        spread(pos, 0, tgt_pos)
        each_other(tab, slot, own_pos, tgt_pos, own, out, one)


def far_kernel(slot, tab, got, got_pos, pos, tens, begun, out, tgt_pos, acc, one):
    acc[...] = begun[...]
    each_apply(tab, 3 + slot, got, tens, acc)
    spread(pos, 0, tgt_pos)
    each_other(tab, 3 + slot, got_pos, tgt_pos, got, acc, one)
    settle(acc, out)


def here_kernel(tab, own, got, own_pos, got_pos, tens, out, acc, one):
    acc[...] = jnp.zeros_like(acc)
    for group, src_pos, dip in ((0, own_pos, own), (3, got_pos, got)):
        each_apply(tab, group, dip, tens, acc)
        each_other(tab, group, src_pos, own_pos, dip, acc, one)
    settle(acc, out)


def first_here_kernel(tab, own, got, own_pos, got_pos, tens_in, out, tens, acc, one):
    each_build(tab, 3, got_pos, own_pos, tens)
    here_kernel(tab, own, got, own_pos, got_pos, tens, out, acc, one)


def respond_rows(alpha, total):
    real_row = lax.broadcasted_iota(jnp.int32, (8, total.shape[1]), 0) % 2 < 1
    turned = jnp.where(real_row, pltpu.roll(total, 7, 0), pltpu.roll(total, 1, 0))
    return alpha[0:8] * total + alpha[8:16] * turned


def update_kernel(field, from_a, from_b, applied, alpha, dip):
    for a in range(3):
        rows = slice(8 * a, 8 * a + 8)
        total = applied[rows, :] + coupling * (field[rows, :] + from_a[rows, :] + from_b[rows, :])
        dip[rows, :] = respond_rows(alpha[...], total)


def last_kernel(field, from_a, from_b, applied, alpha, out):
    for a in range(3):
        rows = slice(8 * a, 8 * a + 8)
        total = applied[rows, :] + coupling * (field[rows, :] + from_a[rows, :] + from_b[rows, :])
        dip = respond_rows(alpha[...], total)
        for s in range(SLABS):
            out[s, a] = dip[2 * s : 2 * s + 2]


def pack_kernel(pos_in, pol_in, field_in, codes_in, count, out, pos, pol, field, codes, sems):
    pairs = ((field_in, field), (pol_in, pol), (pos_in, pos), (codes_in, codes))
    copies = [pltpu.make_async_copy(a, b, sems.at[k]) for k, (a, b) in enumerate(pairs)]
    for copy in copies:
        copy.start()
    for copy in copies:
        copy.wait()
    lane = lax.broadcasted_iota(jnp.int32, (1, BLOCK), 1)
    row = jnp.where(lane == codes.shape[0], count[0], 0)
    for p in range(codes.shape[0]):
        row = jnp.where(lane == p, codes[p], row)
    for f in range(SLABS):
        out[f, 0, 0:2, :] = field[f, 0]
        out[f, 0, 2:4, :] = field[f, 1]
        out[f, 1, 0:2, :] = field[f, 2]
        out[f, 1, 2:4, :] = pol[f]
        out[f, 2, 0:3, :] = pos[...]
        out[f, 2, 3:4, :] = jnp.zeros((1, out.shape[3]), jnp.float32)
        out[f, 2, 3:4, 0:BLOCK] = row.astype(jnp.float32)


def join_kernel(got, applied, alpha, own, pos):
    for s in range(SLABS):
        for a in range(3):
            for i in range(2):
                row = 8 * a + 2 * s + i
                at = 2 * a + i
                applied[row : row + 1, :] = got[s, at // 4, at % 4 : at % 4 + 1, :]
        real, imag = got[s, 1, 2:3, :], got[s, 1, 3:4, :]
        alpha[2 * s : 2 * s + 1, :] = real
        alpha[2 * s + 1 : 2 * s + 2, :] = real
        alpha[8 + 2 * s : 9 + 2 * s, :] = -imag
        alpha[9 + 2 * s : 10 + 2 * s, :] = imag
        pos[3 * s : 3 * s + 3, :] = got[s, 2, 0:3, :]
        own[24 + 3 * s : 27 + 3 * s, :] = got[s, 2, 0:3, :]
        own[36 + s : 37 + s, :] = got[s, 2, 3:4, :]
    for a in range(3):
        rows = slice(8 * a, 8 * a + 8)
        own[rows, :] = respond_rows(alpha[...], applied[rows, :])


def call(body, out_shape, scratch=(), in_specs=None, out_specs=None, aliases=None):
    specs = {} if in_specs is None else {"in_specs": in_specs, "out_specs": out_specs}
    return pl.pallas_call(
        body,
        out_shape=out_shape,
        **specs,
        scratch_shapes=list(scratch),
        input_output_aliases=aliases or {},
        compiler_params=pltpu.CompilerParams(vmem_limit_bytes=6 * 1024 * 1024),
    )


def shards(positions, polarizability, applied_field, pair_codes, pair_counts):
    rows = positions.shape[1]
    f32 = jnp.float32
    arr = lambda *shape: jax.ShapeDtypeStruct((*shape, rows), f32)
    held = lambda *shape: pltpu.VMEM((*shape, rows), f32)
    flip = lambda value: lax.ppermute(value, "gz", swaps(2, True))
    turn = lambda value, first: lax.ppermute(value, "gy", swaps(lax.axis_size("gy"), first))
    keep = lambda value: pltpu.with_memory_space_constraint(value, pltpu.VMEM)
    fixed = lambda value: pltpu.with_memory_space_constraint(value, pltpu.SMEM)
    arguments = (
        positions,
        polarizability,
        jnp.transpose(applied_field, (0, 2, 1, 3)),
        pair_codes,
    )
    sent = call(
        pack_kernel,
        arr(SLABS, 3, 4),
        [pltpu.VMEM(value.shape, f32) for value in arguments[:3]]
        + [pltpu.SMEM(pair_codes.shape, jnp.int32), pltpu.SemaphoreType.DMA((4,))],
        [pl.BlockSpec(memory_space=pltpu.HBM)] * 4 + [SMEM],
        VMEM,
    )(*[pltpu.with_memory_space_constraint(value, pltpu.HBM) for value in arguments], pair_counts)
    got = lax.all_to_all(sent, "gx", 0, 0)
    applied, alpha, own, pos = call(join_kernel, (arr(24), arr(16), arr(40), arr(12)))(got)
    got = flip(own)
    pos_b = turn(pos, False)
    pos_a = turn(pos, True)
    tens_shape = pltpu.VMEM((KEPT, 2 * BLOCK, 6 * BLOCK), jnp.bfloat16)
    one = pltpu.VMEM((1, 2 * BLOCK, 6 * BLOCK), jnp.bfloat16)
    tgt_pos, acc = held(SLABS, 8), held(SLABS, 24)
    tens, tab, own_pos, got_pos = call(
        first_kernel,
        (tens_shape, pltpu.SMEM((12 * STRIDE,), jnp.int32), arr(SLABS, 8), arr(SLABS, 8)),
        (pltpu.SMEM((2 * SLABS, 1, BLOCK), f32), pltpu.SemaphoreType.DMA((2 * SLABS,))),
        [VMEM] * 2,
        (VMEM, SMEM, VMEM, VMEM),
    )(own, got)
    tab = fixed(tab)

    def first_far(slot, pos, tens):
        return call(
            functools.partial(first_far_kernel, slot),
            (arr(24), tens_shape),
            (tgt_pos, acc, one),
            [SMEM] + [VMEM] * 6,
            (VMEM, VMEM),
            {6: 1},
        )(tab, own, got, own_pos, got_pos, pos, keep(tens))

    def here(own, got):
        return call(here_kernel, arr(24), (acc, one), [SMEM] + [VMEM] * 5, VMEM)(
            tab, own, got, own_pos, got_pos, keep(tens)
        )

    def far(slot, got, pos, begun):
        return call(
            functools.partial(far_kernel, slot),
            arr(24),
            (tgt_pos, acc, one),
            [SMEM] + [VMEM] * 5,
            VMEM,
        )(tab, got, got_pos, pos, keep(tens), begun)

    msg_a, tens = first_far(1, pos_a, tens)
    msg_b, tens = first_far(2, pos_b, tens)
    from_b = turn(msg_b, False)
    from_a = turn(msg_a, True)
    field, tens = call(
        first_here_kernel,
        (arr(24), tens_shape),
        (acc, one),
        [SMEM] + [VMEM] * 5,
        (VMEM, VMEM),
        {5: 1},
    )(tab, own, got, own_pos, got_pos, keep(tens))
    for sweep in range(1, ITERS):
        own = call(update_kernel, arr(24))(field, from_a, from_b, applied, alpha)
        got = flip(own)
        at_a, at_b = call(
            own_kernel,
            (arr(SLABS, 24), arr(SLABS, 24)),
            (tgt_pos, one),
            [SMEM] + [VMEM] * 5,
            (VMEM, VMEM),
        )(tab, own, own_pos, pos_a, pos_b, keep(tens))
        from_b = turn(far(2, got, pos_b, at_b), False)
        from_a = turn(far(1, got, pos_a, at_a), True)
        field = here(own, got)
    out = call(last_kernel, arr(SLABS, 3, 2))(field, from_a, from_b, applied, alpha)
    return jnp.transpose(lax.all_to_all(out, "gx", 0, 0), (0, 2, 1, 3))


def solution(mesh):
    in_specs = (
        P(None, ("gx", "gy", "gz")),
        P(None, None, ("gx", "gy", "gz")),
        P(None, None, None, ("gx", "gy", "gz")),
        P(("gx", "gy", "gz")),
        P(("gx", "gy", "gz")),
    )
    out_specs = P(None, None, None, ("gx", "gy", "gz"))
    return jax.shard_map(shards, mesh=mesh, in_specs=in_specs, out_specs=out_specs, check_vma=False)
```
